128 devices in a mesh: side: 2 (over y_hi), dev: 64 (over y_lo, z, x, core).
Axes of the slice: x: 4, y: 4 (y_hi: 2, y_lo: 2; y = y_hi * 2 + y_lo), z: 4, core: 2. Of those that a mesh axis runs over, the one named last changes fastest.
Arguments:
- queries: bfloat16 [2048, 8192], P('dev', 'side'), may hold values from -6 to 6
- cache_keys: bfloat16 [2048, 256, 512], P('dev', None, 'side'), may hold values from -6 to 6
- cache_values: bfloat16 [2048, 256, 512], P('dev', None, 'side'), may hold values from -6 to 6
- new_key: bfloat16 [2048, 512], P('dev', 'side'), may hold values from -15 to 15
- new_value: bfloat16 [2048, 512], P('dev', 'side'), may hold values from -6 to 6
- cache_lengths: int32 [2048], P('dev'), may hold values from 2 to 256, as said below
- hidden: bfloat16 [2048, 4096], P('dev'), may hold values from -6 to 6
- norm_gain: bfloat16 [4096], replicated, may hold values from 0.099609375 to 1.8984375
- expert_ids: int32 [2048, 8], P('dev'), may hold values from 0 to 63, all different within a row; in each aligned block of 32 rows (0 to 31, 32 to 63, ...) at most 8 rows name the same one
- router_probs: float32 [2048, 8], P('dev'), may hold values from 0.02 to 1
- w_gate: bfloat16 [64, 4096, 1536], P('dev', None, 'side'), may hold values from -0.09375 to 0.09375
- w_up: bfloat16 [64, 4096, 1536], P('dev', None, 'side'), may hold values from -0.09375 to 0.09375
- w_down: bfloat16 [64, 1536, 4096], P('dev', 'side'), may hold values from -0.15625 to 0.15625
Outputs:
- context: bfloat16 [2048, 8192], P('dev', 'side')
- moe_out: bfloat16 [2048, 4096], P('dev')
The draws below stay inside these ranges and needn't reach their ends.
Inputs may be any that keep to these rules, and one draw needn't show every extreme that they name: `expert_ids`: in each aligned block of 32 rows (the rows of one dev index) no expert is named more than 8 times, a bound that some block reaches. `cache_lengths`: every aligned block of 32 tokens holds a token with 256 valid positions.
All inputs are finite; a program needn't handle non-finite values.
Results may differ from the reference program's by a relative error of at most 0.012.
Values may be sent and summed in bfloat16 or wider, within the bound.
A program may use at most 128 MiB of HBM per device.

```python
import math
import jax
import jax.numpy as jnp
import numpy as np
from jax import lax

D = 4096
HEADS = 64
KV_HEADS = 4
HEAD_DIM = 128
FF = 1536
TOPK = 8
CACHE = 256
ROWS = 32
EXPERTS = 64
CAP = 8
TOKENS = 2048
N_SIDE = 2
N_DEV = 64


def draw_queries(key, part):
    base = jnp.clip(jax.random.normal(jax.random.fold_in(key, 1), (TOKENS, HEADS * HEAD_DIM), jnp.float32), -5.0, 5.0)
    return base.astype(jnp.bfloat16)


def draw_cache_keys(key, part):
    base = jnp.clip(jax.random.normal(jax.random.fold_in(key, 2), (TOKENS, CACHE, KV_HEADS * HEAD_DIM), jnp.float32), -5.0, 5.0)
    return base.astype(jnp.bfloat16)


def draw_cache_lengths(key, part):
    drawn = jax.random.randint(jax.random.fold_in(key, 3), (TOKENS,), 2, CACHE + 1, dtype=jnp.int32)
    token_index = jnp.arange(TOKENS, dtype=jnp.int32)
    return jnp.where(token_index % ROWS == 5 % ROWS, CACHE, drawn).astype(jnp.int32)


def shard_levels(stream_key, dims, cuts, smallest, largest):
    loudness = 1.0
    for position, shards_of in cuts:
        draws = jax.random.uniform(jax.random.fold_in(jax.random.fold_in(stream_key, 6), position), (shards_of,), jnp.float32, smallest / len(cuts), largest / len(cuts))
        loudness = loudness * jnp.repeat(jnp.exp(draws), dims[position] // shards_of).reshape((-1,) + (1,) * (len(dims) - 1 - position))
    return loudness


def routed_block(rng, own, number, rows, count, top, reach, slope):
    ranking = jax.random.permutation(rng, count)
    heavy_load, ordinary = shares(count, rows * top, reach, slope, True), shares(count, rows * top, reach, slope, False)
    places = jnp.arange(count)

    def named(tallies, turn):
        used = int((tallies > 0).sum())
        fixed = max(1, used // 4)
        moved = fixed + (places - fixed + turn * (used - fixed)) % max(1, count - fixed)
        return jnp.zeros((count,), jnp.int32).at[ranking[jnp.where(places < fixed, places, moved)]].set(jnp.asarray(tallies, jnp.int32))

    tallies = jnp.where(number % 4 == 0, named(heavy_load, number // 4), named(ordinary, number - number // 4 - 1))
    mixed = jax.random.permutation(jax.random.fold_in(own, 3), count)
    source_of, sink = mixed[0:count // 2 * 2:2], mixed[1:count // 2 * 2:2]
    margin = jnp.minimum(tallies[source_of] - 1, reach - tallies[sink]) // 2
    margin = jnp.where((source_of == ranking[0]) | (sink == ranking[0]) | (tallies[sink] == 0), 0, jnp.maximum(margin, 0))
    moved = jax.random.randint(jax.random.fold_in(own, 4), (count // 2,), 0, 1 << 20) % (margin + 1)
    tallies = tallies.at[source_of].add(-moved).at[sink].add(moved)
    items = jnp.searchsorted(jnp.cumsum(tallies), jnp.arange(rows * top), side="right").astype(jnp.int32)
    listing = items.reshape(top, rows).T
    listing = listing[jax.random.permutation(jax.random.fold_in(own, 1), rows)]
    turn = jax.random.randint(jax.random.fold_in(own, 2), (rows, 1), 0, top)
    return jnp.take_along_axis(listing, (jnp.arange(top)[None, :] + turn) % top, axis=1)


def shares(number_of, total, limit, skew, full):
    weights = [(1 << 20) // math.isqrt(grade ** skew) + 1 for grade in range(1, number_of + 1)]
    largest = limit if full else min(limit, max(-(-total // number_of), total * weights[0] // sum(weights)))
    least = 1 if total - largest >= number_of - 1 else 0
    given, rest = [largest] + [least] * (number_of - 1), total - largest - least * (number_of - 1)
    while rest > 0:
        movable = [i for i in range(1, number_of) if given[i] < largest] or [i for i in range(1, number_of) if given[i] < limit]
        pool, budget = sum([weights[i] for i in movable]), rest
        for i in movable:
            more = min(limit - given[i], max(1, budget * weights[i] // pool), rest)
            given[i] = given[i] + more
            rest = rest - more
    return np.array(given)


def noise(key, shape, deviation, limit, pieces=(), kind=jnp.bfloat16):
    values = jax.random.normal(key, shape, jnp.float32) * deviation
    if len(pieces) > 0:
        values = shard_levels(key, shape, pieces, -0.22, 0.18) * values
    return jnp.clip(values, min=-limit, max=limit).astype(kind)


def setup_inputs(seed: int = 0) -> dict:
    splits = jax.random.split(jax.random.key(seed), 14)
    queries = draw_queries(jax.random.fold_in(splits[13], 71), 0)
    cache_keys = draw_cache_keys(jax.random.fold_in(splits[13], 71), 0)
    cache_values = noise(splits[2], (TOKENS, CACHE, KV_HEADS * HEAD_DIM), 1.0, 6.0, ((0, 64), (2, 2)))
    new_key = noise(splits[3], (TOKENS, KV_HEADS * HEAD_DIM), 2.5, 15.0, ((0, 64), (1, 2)))
    new_value = noise(splits[4], (TOKENS, KV_HEADS * HEAD_DIM), 1.0, 6.0, ((0, 64), (1, 2)))
    cache_lengths = draw_cache_lengths(jax.random.fold_in(splits[13], 71), 0)
    hidden = noise(splits[6], (TOKENS, D), 1.0, 6.0, ((0, 64),))
    norm_gain = jnp.clip(1.0 + 0.18 * jax.random.normal(splits[7], (D,), jnp.float32), 0.099609375, 1.8984375).astype(jnp.bfloat16)
    expert_ids_keys = jax.random.split(jax.random.fold_in(splits[8], 1), TOKENS // ROWS)
    expert_ids_turns = jax.random.permutation(jax.random.fold_in(splits[8], 3), TOKENS // ROWS)
    expert_ids = jax.vmap(lambda own, number: routed_block(jax.random.fold_in(splits[8], 2), own, number, ROWS, EXPERTS, TOPK, CAP, 2))(expert_ids_keys, expert_ids_turns).reshape((TOKENS, TOPK))
    router_probs = jnp.clip(jnp.exp(math.log(1.0) - 3.912023 * jax.random.uniform(splits[9], (TOKENS, TOPK), jnp.float32) ** shard_levels(splits[9], (TOKENS, TOPK), ((0, 64),), -0.2, 0.2)), 0.02, 1.0)
    w_gate = noise(splits[10], (EXPERTS, D, FF), D ** -0.5, 0.09375, ((0, 64), (2, 2)))
    w_up = noise(splits[11], (EXPERTS, D, FF), D ** -0.5, 0.09375, ((0, 64), (2, 2)))
    w_down = noise(splits[12], (EXPERTS, FF, D), FF ** -0.5, 0.15625, ((0, 64), (1, 2)))
    return {"queries": queries, "cache_keys": cache_keys, "cache_values": cache_values, "new_key": new_key, "new_value": new_value, "cache_lengths": cache_lengths, "hidden": hidden, "norm_gain": norm_gain, "expert_ids": expert_ids, "router_probs": router_probs, "w_gate": w_gate, "w_up": w_up, "w_down": w_down}


def route_onehot(block_ids, expert_count, capacity):
    flat_ids = block_ids.reshape(-1)
    expert_hot = (flat_ids[:, None] == jnp.arange(expert_count, dtype=jnp.int32)[None, :]).astype(jnp.int32)
    earlier = jnp.cumsum(expert_hot, axis=0) - expert_hot
    slot_rank = lax.optimization_barrier(jnp.sum(earlier * expert_hot, axis=1))
    slot_hot = (slot_rank[:, None] == jnp.arange(capacity, dtype=jnp.int32)[None, :]).astype(jnp.float32)
    route_hot = expert_hot.astype(jnp.float32)[:, :, None] * slot_hot[:, None, :]
    return route_hot.reshape(block_ids.shape[0], block_ids.shape[1], expert_count, capacity)

def attend_block(block_args):
    query_block, key_block, value_block, key_new, value_new, block_lengths = block_args
    row_count = query_block.shape[0]
    per_group = HEADS // KV_HEADS
    score_scale = HEAD_DIM ** (-0.5)
    query_heads = query_block.astype(jnp.float32).reshape(row_count, KV_HEADS, per_group, HEAD_DIM)
    key_heads = key_block.astype(jnp.float32).reshape(row_count, CACHE, KV_HEADS, HEAD_DIM)
    value_heads = value_block.astype(jnp.float32).reshape(row_count, CACHE, KV_HEADS, HEAD_DIM)
    scores = jnp.einsum('tgqd,tlgd->tgql', query_heads, key_heads) * score_scale
    own_key = key_new.astype(jnp.float32).reshape(row_count, KV_HEADS, HEAD_DIM)
    own_score = jnp.einsum('tgqd,tgd->tgq', query_heads, own_key) * score_scale
    visible = jnp.arange(CACHE, dtype=jnp.int32)[None, :] < block_lengths[:, None]
    scores = jnp.where(visible[:, None, None, :], scores, -1e+30)
    top_score = jnp.maximum(lax.optimization_barrier(jnp.max(scores, axis=3)), own_score)
    exp_scores = jnp.exp(scores - top_score[..., None])
    own_exp = jnp.exp(own_score - top_score)
    denominator = lax.optimization_barrier(jnp.sum(exp_scores, axis=3)) + own_exp
    attn_weights = (exp_scores / denominator[..., None]).astype(jnp.bfloat16)
    own_prob = (own_exp / denominator).astype(jnp.bfloat16)
    combined = jnp.einsum('tgql,tlgd->tgqd', attn_weights.astype(jnp.float32), value_heads)
    own_value = value_new.astype(jnp.float32).reshape(row_count, KV_HEADS, 1, HEAD_DIM)
    combined = combined + own_prob.astype(jnp.float32)[..., None] * own_value
    return combined.reshape(row_count, HEADS * HEAD_DIM).astype(jnp.bfloat16)

def by_block(array):
    return array.reshape((N_DEV, ROWS) + array.shape[1:])

def reference(queries, cache_keys, cache_values, new_key, new_value, cache_lengths, hidden, norm_gain, expert_ids, router_probs, w_gate, w_up, w_down):
    context = lax.map(attend_block, (by_block(queries), by_block(cache_keys), by_block(cache_values), by_block(new_key), by_block(new_value), by_block(cache_lengths)))
    context = context.reshape(TOKENS, HEADS * HEAD_DIM)
    gate_share = router_probs / lax.optimization_barrier(jnp.sum(router_probs, axis=1, keepdims=True))
    hidden_wide = hidden.astype(jnp.float32)
    inverse = lax.rsqrt(lax.optimization_barrier(jnp.mean(hidden_wide * hidden_wide, axis=1, keepdims=True)) + 1e-06)
    normed = (hidden_wide * inverse * norm_gain.astype(jnp.float32)[None, :]).astype(jnp.bfloat16)
    block_ids = expert_ids.reshape(N_DEV, ROWS, TOPK)
    block_hot = jax.vmap(route_onehot, in_axes=(0, None, None))(block_ids, EXPERTS, CAP)
    slot_hot = lax.optimization_barrier(jnp.sum(block_hot, axis=2))
    slot_gate = lax.optimization_barrier(jnp.sum(block_hot * gate_share.reshape(N_DEV, ROWS, TOPK)[..., None, None], axis=2))
    buffers = jnp.einsum('nrec,nrd->encd', slot_hot, normed.astype(jnp.float32).reshape(N_DEV, ROWS, D)).astype(jnp.bfloat16)
    expert_gates = jnp.transpose(slot_gate, (2, 0, 1, 3))
    half_width = FF // N_SIDE

    def expert_step(running, expert_items):
        expert_rows, gate_weight, up_weight, down_weight, expert_gate = expert_items
        flat_rows = expert_rows.reshape(N_DEV * CAP, D)
        gate_act = jnp.dot(flat_rows, gate_weight, preferred_element_type=jnp.float32)
        up_act = jnp.dot(flat_rows, up_weight, preferred_element_type=jnp.float32)
        activation = (jax.nn.silu(gate_act) * up_act).astype(jnp.bfloat16)
        summed = jnp.zeros((N_DEV * CAP, D), jnp.float32)
        for half_index in range(N_SIDE):
            low = half_index * half_width
            partial_value = jnp.dot(activation[:, low:low + half_width], down_weight[low:low + half_width], preferred_element_type=jnp.float32).astype(jnp.bfloat16)
            summed = summed + partial_value.astype(jnp.float32)
        summed = summed.reshape(N_DEV, CAP, D)
        running = running + jnp.einsum('nrc,ncd->nrd', expert_gate, summed, precision=lax.Precision.HIGHEST)
        return (running, None)
    running, _ = lax.scan(expert_step, jnp.zeros((N_DEV, ROWS, D), jnp.float32), (buffers, w_gate, w_up, w_down, expert_gates))
    moe_out = running.reshape(TOKENS, D).astype(jnp.bfloat16)
    return (context, moe_out)
```

```python
import functools

import jax
import jax.numpy as jnp
from jax import lax
from jax.experimental import pallas as pl
from jax.experimental.pallas import tpu as pltpu
from jax.sharding import PartitionSpec as P

HEADS = 64
KV_HEADS = 4
HEAD_DIM = 128
RING = 4
BLOCKS = 16
ROWS = 32
SLOTS = 8
GROUPS = 4
D = 4096
HALF = 2048
TAIL = 128
WIDE = HALF + TAIL
MESH = pl.DeviceIdType.MESH
F32 = jnp.float32
BF16 = jnp.bfloat16


class Place:
    def __init__(self):
        self.side = lax.axis_index("side")
        dev = lax.axis_index("dev")
        self.dev = dev
        self.core = dev % 2
        self.x = (dev // 2) % RING
        self.z = (dev // 8) % RING
        self.lo = dev // 32
        self.y = self.side * 2 + self.lo

    @staticmethod
    def index(lo, z, x, core):
        return ((lo * RING + z) * RING + x) * 2 + core

    def plane(self, axis, step):
        if axis == "x":
            return (self.side, self.index(self.lo, self.z, (self.x + step) % RING, self.core))
        return (self.side, self.index(self.lo, (self.z + step) % RING, self.x, self.core))

    def along_y(self, step, core):
        y = (self.y + step) % RING
        return (y // 2, self.index(y % 2, self.z, self.x, core))

    def sibling(self):
        return (self.side, self.index(self.lo, self.z, self.x, 1 - self.core))

    def block(self, half, first, second):
        if half == 0:
            x, z = (self.x + first) % RING, (self.z + second) % RING
        else:
            z, x = (self.z + first) % RING, (self.x + second) % RING
        return z * RING + x


AXES = (("x", "z"), ("z", "x"))
NEAR = (0, -1, 1, 2)


def greet(devices):
    barrier = pltpu.get_barrier_semaphore()
    for device in devices:
        pl.semaphore_signal(barrier, inc=1, device_id=device, device_id_type=MESH)
    pl.semaphore_wait(barrier, len(devices))


def routing_table(ids_ref, probs_ref):
    lane = lax.broadcasted_iota(jnp.int32, (ROWS, TAIL), 1)
    expert = lane % 64
    ids = ids_ref[...]
    probs = probs_ref[...]
    share = probs / jnp.sum(probs, axis=1, keepdims=True)
    hit = jnp.zeros((ROWS, TAIL), F32)
    gate = jnp.zeros((ROWS, TAIL), F32)
    for k in range(ids.shape[1]):
        match = ids[:, k : k + 1] == expert
        hit = jnp.where(match, 1.0, hit)
        gate = jnp.where(match, share[:, k : k + 1], gate)
    row = lax.broadcasted_iota(jnp.int32, (ROWS, ROWS), 0)
    col = lax.broadcasted_iota(jnp.int32, (ROWS, ROWS), 1)
    before = jnp.where(col < row, 1.0, 0.0).astype(BF16)
    rank = jnp.dot(before, hit.astype(BF16), preferred_element_type=F32)
    rank = jnp.where(hit > 0.5, rank, 100.0)
    lead = gate.astype(BF16)
    trail = (gate - lead.astype(F32)).astype(BF16)
    left = lane < 64
    rank = rank.astype(BF16)
    return jnp.where(left, rank, lead), jnp.where(left, rank, trail)


def dispatch_kernel(
    hidden_ref, gain_ref, ids_ref, probs_ref, x_ref, weight_ref,
    gathered, picked_y, picked_s, ag_send, ag_recv, pick_send, x_recv,
):
    me = Place()
    own_group = me.lo * 2 + me.core

    wide = hidden_ref[...].astype(F32)
    inverse = lax.rsqrt(jnp.mean(wide * wide, axis=1, keepdims=True) + 1e-06)
    normed = (wide * inverse * gain_ref[...].astype(F32)).astype(BF16)
    tables = routing_table(ids_ref, probs_ref)
    own_block = me.block(0, 0, 0)
    for half in range(2):
        gathered[half, own_block, :, 0:HALF] = normed[:, half * HALF : (half + 1) * HALF]
        gathered[half, own_block, :, HALF:WIDE] = tables[half]

    lo = 1 - me.lo
    experts = (
        me.dev,
        me.index(me.lo, me.z, me.x, 1 - me.core),
        me.index(lo, me.z, me.x, 0),
        me.index(lo, me.z, me.x, 1),
    )
    slot_of = lax.broadcasted_iota(jnp.int32, (GROUPS * SLOTS, TAIL), 0)
    lane = lax.broadcasted_iota(jnp.int32, (GROUPS * SLOTS, TAIL), 1)
    wanted = jnp.zeros((GROUPS * SLOTS, TAIL), jnp.int32)
    for j in range(GROUPS):
        wanted = jnp.where(slot_of // SLOTS == j, experts[j], wanted)
    pick_rank = jnp.where(lane == wanted, 1.0, 0.0).astype(BF16)
    pick_gate = jnp.where(lane == wanted + 64, 1.0, 0.0).astype(BF16)

    greet(
        [me.plane(axis, step) for axis in ("x", "z") for step in (-1, 1)]
        + [me.along_y(step, core) for step in (-1, 1) for core in (0, 1)]
        + [me.sibling()]
    )

    def hop(half, block, rows, stage, step, sem):
        ref = gathered.at[half, block, rows]
        return pltpu.make_async_remote_copy(
            src_ref=ref, dst_ref=ref, send_sem=ag_send, recv_sem=ag_recv.at[half, sem],
            device_id=me.plane(AXES[half][stage], step), device_id_type=MESH,
        )

    full, low, high = pl.ds(0, ROWS), pl.ds(0, ROWS // 2), pl.ds(ROWS // 2, ROWS // 2)

    def send_both(half, first, stage, base):
        block = me.block(half, first, 0)
        hop(half, block, full, stage, 1, base).start()
        hop(half, block, full, stage, -1, base + 1).start()

    def arrive(half, block, rows, sem):
        ref = gathered.at[half, block, rows]
        pltpu.make_async_copy(ref, ref, ag_recv.at[half, sem]).wait()

    def take_full(half, first, second, stage, base):
        ahead = 1 if stage == 0 else 0
        for step, rows, sem in ((-1, low, base), (1, high, base + 1)):
            block = me.block(half, step, 0) if ahead else me.block(half, first, step)
            arrive(half, block, full, sem)
            hop(half, block, rows, stage, -step, sem + 2).start()

    def take_far(half, first, stage, base):
        block = me.block(half, 2, 0) if stage == 0 else me.block(half, first, 2)
        arrive(half, block, low, base + 2)
        arrive(half, block, high, base + 3)

    def select(half, first, second):
        block = me.block(half, first, second)
        table = gathered[half, block, :, HALF:WIDE]
        rank = lax.dot_general(pick_rank, table, (((1,), (1,)), ((), ())), preferred_element_type=F32)
        slot = (lax.broadcasted_iota(jnp.int32, (GROUPS * SLOTS, ROWS), 0) % SLOTS).astype(F32)
        hot = jnp.where(rank == slot, 1.0, 0.0).astype(BF16)
        chosen = jnp.dot(hot, gathered[half, block, :, 0:HALF], preferred_element_type=F32).astype(BF16)
        columns = pl.ds(half * HALF, HALF)
        x_ref[own_group, block, :, columns] = chosen[0:8]
        picked_s[half, block] = chosen[8:16]
        picked_y[half, block, 0] = chosen[16:24]
        picked_y[half, block, 1] = chosen[24:32]
        for core in range(2):
            pltpu.make_async_remote_copy(
                src_ref=picked_y.at[half, block, core],
                dst_ref=x_ref.at[own_group, block, :, columns],
                send_sem=pick_send, recv_sem=x_recv,
                device_id=me.along_y(1 if half == 0 else -1, core), device_id_type=MESH,
            ).start()
        pltpu.make_async_remote_copy(
            src_ref=picked_s.at[half, block],
            dst_ref=x_ref.at[own_group, block, :, columns],
            send_sem=pick_send, recv_sem=x_recv,
            device_id=me.sibling(), device_id_type=MESH,
        ).start()

    both = range(2)
    for half in both:
        send_both(half, 0, 0, 0)
    for half in both:
        send_both(half, 0, 1, 4)
    for half in both:
        select(half, 0, 0)
    for half in both:
        take_full(half, 0, 0, 0, 0)
        send_both(half, -1, 1, 8)
        send_both(half, 1, 1, 12)
    for half in both:
        select(half, -1, 0)
        select(half, 1, 0)
    for half in both:
        take_full(half, 0, 0, 1, 4)
    for half in both:
        take_far(half, 0, 0, 0)
        send_both(half, 2, 1, 16)
    for half in both:
        select(half, 0, -1)
        select(half, 0, 1)
        select(half, 2, 0)
    for index in range(1, 4):
        first = NEAR[index]
        for half in both:
            take_full(half, first, 0, 1, 4 + 4 * index)
        for half in both:
            take_far(half, NEAR[index - 1], 1, 4 * index)
        for half in both:
            select(half, NEAR[index - 1], 2)
            select(half, first, -1)
            select(half, first, 1)
    for half in both:
        take_far(half, 2, 1, 16)
        select(half, 2, 2)

    for block in range(BLOCKS):
        rank = lax.dot_general(
            gathered[0, block, :, HALF:WIDE], pick_rank, (((1,), (1,)), ((), ())), preferred_element_type=F32
        )
        gate = sum(
            lax.dot_general(
                gathered[half, block, :, HALF:WIDE], pick_gate, (((1,), (1,)), ((), ())), preferred_element_type=F32
            )
            for half in both
        )
        slot = (lax.broadcasted_iota(jnp.int32, (ROWS, GROUPS * SLOTS), 1) % SLOTS).astype(F32)
        weight_ref[block] = jnp.where(rank == slot, gate, 0.0)

    sent = gathered.at[:, pl.ds(0, 15)]
    pltpu.make_async_copy(sent, sent, ag_send).wait()
    picked = picked_y.at[...]
    pltpu.make_async_copy(picked, picked, pick_send).wait()
    picked = picked_s.at[...]
    pltpu.make_async_copy(picked, picked, pick_send).wait()
    came = x_ref.at[pl.ds(0, 3)]
    pltpu.make_async_copy(came, came, x_recv).wait()


def dispatch(hidden, gain, ids, probs):
    vmem = pl.BlockSpec(memory_space=pltpu.VMEM)
    return pl.pallas_call(
        dispatch_kernel,
        out_shape=(
            jax.ShapeDtypeStruct((GROUPS, BLOCKS, SLOTS, D), BF16),
            jax.ShapeDtypeStruct((BLOCKS, ROWS, GROUPS * SLOTS), F32),
        ),
        in_specs=[vmem] * 4,
        out_specs=(vmem, vmem),
        scratch_shapes=[
            pltpu.VMEM((2, BLOCKS, ROWS, WIDE), BF16),
            pltpu.VMEM((2, BLOCKS, 2, SLOTS, HALF), BF16),
            pltpu.VMEM((2, BLOCKS, SLOTS, HALF), BF16),
            pltpu.SemaphoreType.DMA,
            pltpu.SemaphoreType.DMA((2, 20)),
            pltpu.SemaphoreType.DMA,
            pltpu.SemaphoreType.DMA,
        ],
        compiler_params=pltpu.CompilerParams(
            collective_id=0, has_side_effects=True, vmem_limit_bytes=40 * 1024 * 1024
        ),
        name="dispatch",
    )(hidden, gain, ids, probs)


def combine_kernel(
    out_ref_in, weight_ref, moe_ref,
    landed, far2_out, near2_out, far2_in, near2_in, far1_out, near1_out, far1_in, near1_in,
    side_out, side_in,
    land_send, land_recv, ring_send, far2_recv, near2_recv, far1_recv, near1_recv, side_send, side_recv,
):
    me = Place()
    lo = 1 - me.lo
    both = range(2)
    order = (2, 1, -1, 0)
    step2 = (2, 1, -1, 0)

    other_side = (1 - me.side, me.dev)
    greet(
        [me.plane(axis, step) for axis in ("x", "z") for step in (-1, 1)]
        + [me.along_y(step, core) for step in (-1, 1) for core in (0, 1)]
        + [me.sibling(), other_side]
    )

    for first in order:
        for second in step2:
            for half in both:
                block = me.block(half, first, second)
                columns = pl.ds(half * HALF, HALF)
                for core in range(2):
                    pltpu.make_async_remote_copy(
                        src_ref=out_ref_in.at[lo * 2 + core, block, :, columns],
                        dst_ref=landed.at[half, block, 1 + me.core],
                        send_sem=land_send, recv_sem=land_recv.at[half, block],
                        device_id=me.along_y(1 if half == 0 else -1, core), device_id_type=MESH,
                    ).start()
                pltpu.make_async_remote_copy(
                    src_ref=out_ref_in.at[me.lo * 2 + 1 - me.core, block, :, columns],
                    dst_ref=landed.at[half, block, 0],
                    send_sem=land_send, recv_sem=land_recv.at[half, block],
                    device_id=me.sibling(), device_id_type=MESH,
                ).start()

    own_group = me.lo * 2 + me.core

    def mixed(half, first, second):
        block = me.block(half, first, second)
        ref = landed.at[half, block]
        pltpu.make_async_copy(ref, ref, land_recv.at[half, block]).wait()
        weight = weight_ref[block]
        lead = weight.astype(BF16)
        trail = (weight - lead.astype(F32)).astype(BF16)
        own = out_ref_in[own_group, block, :, pl.ds(half * HALF, HALF)]
        parts = landed[half, block]
        rows = jnp.concatenate([own, parts[0], parts[1], parts[2]], axis=0)
        return jnp.dot(lead, rows, preferred_element_type=F32) + jnp.dot(trail, rows, preferred_element_type=F32)

    def ring(half, stage, step, src, dst, sem):
        pltpu.make_async_remote_copy(
            src_ref=src, dst_ref=dst, send_sem=ring_send, recv_sem=sem,
            device_id=me.plane(AXES[half][stage], step), device_id_type=MESH,
        ).start()

    def arrive(ref, sem):
        pltpu.make_async_copy(ref, ref, sem).wait()

    low, high = slice(0, ROWS // 2), slice(ROWS // 2, ROWS)
    def send_far(half, stage, value, out, into, sems):
        out[...] = value.astype(BF16)
        for way, step, rows in ((0, 1, pl.ds(0, 16)), (1, -1, pl.ds(16, 16))):
            ring(half, stage, step, out.at[rows], into.at[way], sems(way))

    def send_near(half, stage, way, value, far_in, far_sem, out, into, sem):
        arrive(far_in, far_sem)
        passed = far_in[...].astype(F32)
        if way == 0:
            out[low] = (value[low] + passed).astype(BF16)
            out[high] = value[high].astype(BF16)
        else:
            out[low] = value[low].astype(BF16)
            out[high] = (value[high] + passed).astype(BF16)
        ring(half, stage, 1 if way == 0 else -1, out, into, sem)

    def far2(half, index):
        value = mixed(half, order[index], 2)
        send_far(
            half, 1, value, far2_out.at[half, index], far2_in.at[half, index],
            lambda way: far2_recv.at[half, index, way],
        )

    def near2(half, index):
        for way, second in ((0, 1), (1, -1)):
            value = mixed(half, order[index], second)
            send_near(
                half, 1, way, value, far2_in.at[half, index, way], far2_recv.at[half, index, way],
                near2_out.at[half, index, way], near2_in.at[half, index, way], near2_recv.at[half, index, way],
            )

    def total2(half, index):
        value = mixed(half, order[index], 0)
        for way in range(2):
            arrive(near2_in.at[half, index, way], near2_recv.at[half, index, way])
            value = value + near2_in[half, index, way].astype(F32)
        return value

    def stage1(half, index):
        value = total2(half, index)
        first = order[index]
        if first == 2:
            send_far(
                half, 0, value, far1_out.at[half], far1_in.at[half], lambda way: far1_recv.at[half, way]
            )
        elif first != 0:
            way = 0 if first == 1 else 1
            send_near(
                half, 0, way, value, far1_in.at[half, way], far1_recv.at[half, way],
                near1_out.at[half, way], near1_in.at[half, way], near1_recv.at[half, way],
            )
        else:
            for way in range(2):
                arrive(near1_in.at[half, way], near1_recv.at[half, way])
                value = value + near1_in[half, way].astype(F32)
            side_out[half] = value.astype(BF16)
            pltpu.make_async_remote_copy(
                src_ref=side_out.at[half], dst_ref=side_in.at[half],
                send_sem=side_send, recv_sem=side_recv.at[half],
                device_id=other_side, device_id_type=MESH,
            ).start()

    for half in both:
        far2(half, 0)
    for index in range(4):
        if index < 3:
            for half in both:
                far2(half, index + 1)
        for half in both:
            near2(half, index)
        if index > 0:
            for half in both:
                stage1(half, index - 1)
    for half in both:
        stage1(half, 3)
    for half in both:
        arrive(side_in.at[half], side_recv.at[half])
        moe_ref[:, half * HALF : (half + 1) * HALF] = (
            side_out[half].astype(F32) + side_in[half].astype(F32)
        ).astype(BF16)

    came = out_ref_in.at[pl.ds(0, 3)]
    pltpu.make_async_copy(came, came, land_send).wait()
    for ref in (far2_out, near2_out, far1_out, near1_out):
        pltpu.make_async_copy(ref, ref, ring_send).wait()
    pltpu.make_async_copy(side_out, side_out, side_send).wait()


def combine(expert_out, weight):
    vmem = pl.BlockSpec(memory_space=pltpu.VMEM)
    dma = pltpu.SemaphoreType.DMA
    return pl.pallas_call(
        combine_kernel,
        out_shape=jax.ShapeDtypeStruct((ROWS, D), BF16),
        in_specs=[vmem] * 2,
        out_specs=vmem,
        scratch_shapes=[
            pltpu.VMEM((2, BLOCKS, 3, SLOTS, HALF), BF16),
            pltpu.VMEM((2, 4, ROWS, HALF), BF16),
            pltpu.VMEM((2, 4, 2, ROWS, HALF), BF16),
            pltpu.VMEM((2, 4, 2, ROWS // 2, HALF), BF16),
            pltpu.VMEM((2, 4, 2, ROWS, HALF), BF16),
            pltpu.VMEM((2, ROWS, HALF), BF16),
            pltpu.VMEM((2, 2, ROWS, HALF), BF16),
            pltpu.VMEM((2, 2, ROWS // 2, HALF), BF16),
            pltpu.VMEM((2, 2, ROWS, HALF), BF16),
            pltpu.VMEM((2, ROWS, HALF), BF16),
            pltpu.VMEM((2, ROWS, HALF), BF16),
            dma, dma((2, BLOCKS)), dma, dma((2, 4, 2)), dma((2, 4, 2)), dma((2, 2)), dma((2, 2)), dma, dma((2,)),
        ],
        compiler_params=pltpu.CompilerParams(
            collective_id=1, has_side_effects=True, vmem_limit_bytes=48 * 1024 * 1024
        ),
        name="combine",
    )(expert_out, weight)


def attend_local(queries, cache_keys, cache_values, new_key, new_value, cache_lengths):
    row_count = queries.shape[0]
    cache_len = cache_keys.shape[1]
    groups = cache_keys.shape[2] // HEAD_DIM
    per_group = HEADS // KV_HEADS
    score_scale = HEAD_DIM ** (-0.5)
    query_heads = queries.reshape(row_count, groups, per_group, HEAD_DIM)
    key_heads = cache_keys.reshape(row_count, cache_len, groups, HEAD_DIM)
    value_heads = cache_values.reshape(row_count, cache_len, groups, HEAD_DIM)
    scores = (
        jnp.einsum("tgqd,tlgd->tgql", query_heads, key_heads, preferred_element_type=jnp.float32)
        * score_scale
    )
    own_key = new_key.reshape(row_count, groups, HEAD_DIM)
    own_score = (
        jnp.einsum("tgqd,tgd->tgq", query_heads, own_key, preferred_element_type=jnp.float32)
        * score_scale
    )
    visible = jnp.arange(cache_len, dtype=jnp.int32)[None, :] < cache_lengths[:, None]
    scores = jnp.where(visible[:, None, None, :], scores, -1e30)
    top_score = jnp.maximum(jnp.max(scores, axis=3), own_score)
    exp_scores = jnp.exp(scores - top_score[..., None])
    own_exp = jnp.exp(own_score - top_score)
    denominator = jnp.sum(exp_scores, axis=3) + own_exp
    attn_weights = (exp_scores / denominator[..., None]).astype(jnp.bfloat16)
    own_prob = (own_exp / denominator).astype(jnp.bfloat16)
    combined = jnp.einsum(
        "tgql,tlgd->tgqd", attn_weights, value_heads, preferred_element_type=jnp.float32
    )
    own_value = new_value.reshape(row_count, groups, 1, HEAD_DIM).astype(jnp.float32)
    combined = combined + own_prob.astype(jnp.float32)[..., None] * own_value
    return combined.reshape(row_count, groups * per_group * HEAD_DIM).astype(jnp.bfloat16)


def per_device(
    queries,
    cache_keys,
    cache_values,
    new_key,
    new_value,
    cache_lengths,
    hidden,
    norm_gain,
    expert_ids,
    router_probs,
    w_gate,
    w_up,
    w_down,
):
    context = attend_local(queries, cache_keys, cache_values, new_key, new_value, cache_lengths)
    rows, weight = dispatch(hidden, norm_gain.reshape(1, D), expert_ids, router_probs)
    rows = rows.reshape(GROUPS * BLOCKS * SLOTS, D)
    gate_act = jnp.dot(rows, w_gate[0], preferred_element_type=jnp.float32)
    up_act = jnp.dot(rows, w_up[0], preferred_element_type=jnp.float32)
    activation = (jax.nn.silu(gate_act) * up_act).astype(jnp.bfloat16)
    partial_out = jnp.dot(activation, w_down[0], preferred_element_type=jnp.float32).astype(jnp.bfloat16)
    moe_out = combine(partial_out.reshape(GROUPS, BLOCKS, SLOTS, D), weight)
    return (context, moe_out)


def solution(mesh):
    in_specs = (
        P("dev", "side"),
        P("dev", None, "side"),
        P("dev", None, "side"),
        P("dev", "side"),
        P("dev", "side"),
        P("dev"),
        P("dev", None),
        P(),
        P("dev", None),
        P("dev", None),
        P("dev", None, "side"),
        P("dev", None, "side"),
        P("dev", "side", None),
    )
    out_specs = (P("dev", "side"), P("dev", None))
    return jax.shard_map(
        per_device, mesh=mesh, in_specs=in_specs, out_specs=out_specs, check_vma=False
    )
```

```python
import functools

import jax
import jax.numpy as jnp
from jax import lax
from jax.experimental import pallas as pl
from jax.experimental.pallas import tpu as pltpu
from jax.sharding import PartitionSpec as P

HEADS = 64
KV_HEADS = 4
HEAD_DIM = 128
RING = 4
BLOCKS = 16
ROWS = 32
SLOTS = 8
GROUPS = 4
D = 4096
HALF = 2048
TAIL = 128
WIDE = HALF + TAIL
MESH = pl.DeviceIdType.MESH
F32 = jnp.float32
BF16 = jnp.bfloat16


class Place:
    def __init__(self):
        self.side = lax.axis_index("side")
        dev = lax.axis_index("dev")
        self.dev = dev
        self.core = dev % 2
        self.x = (dev // 2) % RING
        self.z = (dev // 8) % RING
        self.lo = dev // 32
        self.y = self.side * 2 + self.lo

    @staticmethod
    def index(lo, z, x, core):
        return ((lo * RING + z) * RING + x) * 2 + core

    def plane(self, axis, step):
        if axis == "x":
            return (self.side, self.index(self.lo, self.z, (self.x + step) % RING, self.core))
        return (self.side, self.index(self.lo, (self.z + step) % RING, self.x, self.core))

    def along_y(self, step, core):
        y = (self.y + step) % RING
        return (y // 2, self.index(y % 2, self.z, self.x, core))

    def sibling(self):
        return (self.side, self.index(self.lo, self.z, self.x, 1 - self.core))

    def block(self, half, first, second):
        if half == 0:
            x, z = (self.x + first) % RING, (self.z + second) % RING
        else:
            z, x = (self.z + first) % RING, (self.x + second) % RING
        return z * RING + x


AXES = (("x", "z"), ("z", "x"))
NEAR = (0, -1, 1, 2)


def routing_table(ids_ref, probs_ref):
    lane = lax.broadcasted_iota(jnp.int32, (ROWS, TAIL), 1)
    expert = lane % 64
    ids = ids_ref[...]
    probs = probs_ref[...]
    share = probs / jnp.sum(probs, axis=1, keepdims=True)
    hit = jnp.zeros((ROWS, TAIL), F32)
    gate = jnp.zeros((ROWS, TAIL), F32)
    for k in range(ids.shape[1]):
        match = ids[:, k : k + 1] == expert
        hit = jnp.where(match, 1.0, hit)
        gate = jnp.where(match, share[:, k : k + 1], gate)
    row = lax.broadcasted_iota(jnp.int32, (ROWS, ROWS), 0)
    col = lax.broadcasted_iota(jnp.int32, (ROWS, ROWS), 1)
    before = jnp.where(col < row, 1.0, 0.0).astype(BF16)
    rank = jnp.dot(before, hit.astype(BF16), preferred_element_type=F32)
    rank = jnp.where(hit > 0.5, rank, 100.0)
    lead = gate.astype(BF16)
    trail = (gate - lead.astype(F32)).astype(BF16)
    left = lane < 64
    rank = rank.astype(BF16)
    return jnp.where(left, rank, lead), jnp.where(left, rank, trail)


CHUNK = 4
KEYS = 256
HIDDEN = 768


def step_kernel(
    hidden_ref, gain_ref, ids_ref, probs_ref, lengths_ref, queries_ref, new_key_ref, new_value_ref,
    keys_hbm, values_hbm, w_gate_hbm, w_up_hbm, w_down_hbm,
    context_ref, moe_ref,
    gathered, picked_y, picked_s, rows_in, weights, w_gate, w_up, w_down, active, rows_out,
    landed, far2_out, near2_out, far2_in, near2_in, far1_out, near1_out, far1_in, near1_in,
    side_out, side_in, keys, values,
    ag_send, ag_recv, pick_send, rows_recv, w_sem, kv_sem,
    land_send, land_recv, ring_send, far2_recv, near2_recv, far1_recv, near1_recv, side_send, side_recv,
):
    me = Place()
    both = range(2)
    lo = 1 - me.lo
    own_group = me.lo * 2 + me.core
    other_side = (1 - me.side, me.dev)

    w_copies = [
        pltpu.make_async_copy(w_gate_hbm, w_gate, w_sem.at[0]),
        pltpu.make_async_copy(w_up_hbm, w_up, w_sem.at[1]),
        pltpu.make_async_copy(w_down_hbm, w_down, w_sem.at[2]),
    ]

    def cache_copies(chunk):
        tokens = pl.ds(chunk * CHUNK, CHUNK)
        slot = chunk % 2
        return (
            pltpu.make_async_copy(keys_hbm.at[tokens], keys.at[slot], kv_sem.at[slot, 0]),
            pltpu.make_async_copy(values_hbm.at[tokens], values.at[slot], kv_sem.at[slot, 1]),
        )

    for chunk in range(2):
        for copy in cache_copies(chunk):
            copy.start()
    for copy in w_copies:
        copy.start()

    neighbours = (
        [me.plane(axis, step) for axis in ("x", "z") for step in (-1, 1)]
        + [me.along_y(step, core) for step in (-1, 1) for core in (0, 1)]
        + [me.sibling(), other_side]
    )
    barrier = pltpu.get_barrier_semaphore()
    for device in neighbours:
        pl.semaphore_signal(barrier, inc=1, device_id=device, device_id_type=MESH)

    wide = hidden_ref[...].astype(F32)
    inverse = lax.rsqrt(jnp.mean(wide * wide, axis=1, keepdims=True) + 1e-06)
    normed = (wide * inverse * gain_ref[...].astype(F32)).astype(BF16)
    tables = routing_table(ids_ref, probs_ref)
    own_block = me.block(0, 0, 0)
    for half in both:
        gathered[half, own_block, :, 0:HALF] = normed[:, half * HALF : (half + 1) * HALF]
        gathered[half, own_block, :, HALF:WIDE] = tables[half]

    experts = (
        me.dev,
        me.index(me.lo, me.z, me.x, 1 - me.core),
        me.index(lo, me.z, me.x, 0),
        me.index(lo, me.z, me.x, 1),
    )
    slot_of = lax.broadcasted_iota(jnp.int32, (GROUPS * SLOTS, TAIL), 0)
    lane = lax.broadcasted_iota(jnp.int32, (GROUPS * SLOTS, TAIL), 1)
    wanted = jnp.zeros((GROUPS * SLOTS, TAIL), jnp.int32)
    for j in range(GROUPS):
        wanted = jnp.where(slot_of // SLOTS == j, experts[j], wanted)
    pick_rank = jnp.where(lane == wanted, 1.0, 0.0).astype(BF16)
    pick_gate = jnp.where(lane == wanted + 64, 1.0, 0.0).astype(BF16)

    pl.semaphore_wait(barrier, len(neighbours))

    def hop(half, block, rows, stage, step, sem):
        ref = gathered.at[half, block, rows]
        return pltpu.make_async_remote_copy(
            src_ref=ref, dst_ref=ref, send_sem=ag_send, recv_sem=ag_recv.at[half, sem],
            device_id=me.plane(AXES[half][stage], step), device_id_type=MESH,
        )

    full, low_rows, high_rows = pl.ds(0, ROWS), pl.ds(0, ROWS // 2), pl.ds(ROWS // 2, ROWS // 2)

    def send_both(half, first, stage, base):
        block = me.block(half, first, 0)
        hop(half, block, full, stage, 1, base).start()
        hop(half, block, full, stage, -1, base + 1).start()

    def landing(ref, sem):
        pltpu.make_async_copy(ref, ref, sem).wait()

    def take_full(half, first, stage, base):
        for step, rows, sem in ((-1, low_rows, base), (1, high_rows, base + 1)):
            block = me.block(half, step, 0) if stage == 0 else me.block(half, first, step)
            landing(gathered.at[half, block], ag_recv.at[half, sem])
            hop(half, block, rows, stage, -step, sem + 2).start()

    def take_far(half, first, stage, base):
        block = me.block(half, 2, 0) if stage == 0 else me.block(half, first, 2)
        landing(gathered.at[half, block, low_rows], ag_recv.at[half, base + 2])
        landing(gathered.at[half, block, high_rows], ag_recv.at[half, base + 3])

    def select(half, first, second):
        block = me.block(half, first, second)
        table = gathered[half, block, :, HALF:WIDE]
        rank = lax.dot_general(pick_rank, table, (((1,), (1,)), ((), ())), preferred_element_type=F32)
        slot = (lax.broadcasted_iota(jnp.int32, (GROUPS * SLOTS, ROWS), 0) % SLOTS).astype(F32)
        hot = jnp.where(rank == slot, 1.0, 0.0).astype(BF16)
        chosen = jnp.dot(hot, gathered[half, block, :, 0:HALF], preferred_element_type=F32).astype(BF16)
        columns = pl.ds(half * HALF, HALF)
        for core in range(2):
            picked_y[half, block, core] = chosen[16 + 8 * core : 24 + 8 * core]
            pltpu.make_async_remote_copy(
                src_ref=picked_y.at[half, block, core],
                dst_ref=rows_in.at[own_group, block, :, columns],
                send_sem=pick_send, recv_sem=rows_recv,
                device_id=me.along_y(1 if half == 0 else -1, core), device_id_type=MESH,
            ).start()
        picked_s[half, block] = chosen[8:16]
        pltpu.make_async_remote_copy(
            src_ref=picked_s.at[half, block],
            dst_ref=rows_in.at[own_group, block, :, columns],
            send_sem=pick_send, recv_sem=rows_recv,
            device_id=me.sibling(), device_id_type=MESH,
        ).start()
        rows_in[own_group, block, :, columns] = chosen[0:8]

    def attend(chunk):
        slot = chunk % 2
        for copy in cache_copies(chunk):
            copy.wait()
        scale = HEAD_DIM ** (-0.5)
        position = lax.broadcasted_iota(jnp.int32, (16, KEYS), 1)
        for item in range(CHUNK):
            token = chunk * CHUNK + item
            visible = position < lengths_ref[token]
            for group in range(2):
                heads = slice(group * 16, (group + 1) * 16)
                lanes = slice(group * HEAD_DIM, (group + 1) * HEAD_DIM)
                query = queries_ref[token, heads]
                scores = lax.dot_general(
                    query, keys[slot, item, :, lanes], (((1,), (1,)), ((), ())), preferred_element_type=F32
                )
                scores = jnp.where(visible, scores * scale, -1e30)
                own_key = new_key_ref[token : token + 1, lanes].astype(F32)
                own = jnp.sum(query.astype(F32) * own_key, axis=1, keepdims=True) * scale
                top = jnp.maximum(jnp.max(scores, axis=1, keepdims=True), own)
                scores = jnp.exp(scores - top)
                own = jnp.exp(own - top)
                total = jnp.sum(scores, axis=1, keepdims=True) + own
                probs = (scores / total).astype(BF16)
                own = (own / total).astype(BF16).astype(F32)
                mixed = jnp.dot(probs, values[slot, item, :, lanes], preferred_element_type=F32)
                mixed = mixed + own * new_value_ref[token : token + 1, lanes].astype(F32)
                context_ref[token, heads] = mixed.astype(BF16)
        if chunk + 2 < ROWS // CHUNK:
            for copy in cache_copies(chunk + 2):
                copy.start()

    for half in both:
        send_both(half, 0, 0, 0)
    for half in both:
        send_both(half, 0, 1, 4)
    for half in both:
        select(half, 0, 0)
    attend(0)
    for half in both:
        take_full(half, 0, 0, 0)
        send_both(half, -1, 1, 8)
    for half in both:
        select(half, -1, 0)
        select(half, 1, 0)
    attend(1)
    for half in both:
        take_full(half, 0, 1, 4)
        send_both(half, 1, 1, 12)
    for half in both:
        take_far(half, 0, 0, 0)
    for half in both:
        select(half, 2, 0)
        select(half, 0, -1)
        select(half, 0, 1)
    attend(2)
    for index in range(1, 4):
        first = NEAR[index]
        for half in both:
            take_full(half, first, 1, 4 + 4 * index)
            if index == 1:
                send_both(half, 2, 1, 16)
        for half in both:
            take_far(half, NEAR[index - 1], 1, 4 * index)
        for half in both:
            select(half, first, -1)
            select(half, first, 1)
            select(half, NEAR[index - 1], 2)
        attend(2 + index)
    for half in both:
        take_far(half, 2, 1, 16)
        select(half, 2, 2)
    attend(6)

    for block in range(BLOCKS):
        rank = lax.dot_general(
            gathered[0, block, :, HALF:WIDE], pick_rank, (((1,), (1,)), ((), ())), preferred_element_type=F32
        )
        gate = sum(
            lax.dot_general(
                gathered[half, block, :, HALF:WIDE], pick_gate, (((1,), (1,)), ((), ())), preferred_element_type=F32
            )
            for half in both
        )
        slot = (lax.broadcasted_iota(jnp.int32, (ROWS, GROUPS * SLOTS), 1) % SLOTS).astype(F32)
        weights[block] = jnp.where(rank == slot, gate, 0.0)
    attend(7)

    for copy in w_copies:
        copy.wait()
    landing(rows_in.at[pl.ds(0, 3)], rows_recv)

    def expert(base):
        rows = rows_in[pl.ds(base, 2)].reshape(2 * BLOCKS * SLOTS, D)
        for low in range(0, HIDDEN, 256):
            columns = slice(low, low + 256)
            gate = jnp.dot(rows, w_gate[:, columns], preferred_element_type=F32)
            up = jnp.dot(rows, w_up[:, columns], preferred_element_type=F32)
            active[:, columns] = (gate / (1.0 + jnp.exp(-gate)) * up).astype(BF16)

    def expert_down(base, half):
        for low in range(half * HALF, (half + 1) * HALF, 512):
            columns = slice(low, low + 512)
            out = jnp.dot(active[...], w_down[:, columns], preferred_element_type=F32).astype(BF16)
            rows_out[pl.ds(base, 2), :, :, columns] = out.reshape(2, BLOCKS, SLOTS, 512)

    far_order = (2, 1, -1, 0)
    visits = (
        (2, 2), (1, 2), (2, 1), (2, -1), (-1, 2), (1, 1), (1, -1), (2, 0),
        (0, 2), (-1, 1), (-1, -1), (1, 0), (0, 1), (0, -1), (-1, 0), (0, 0),
    )

    def give_y(half, visit):
        block = me.block(half, *visits[visit])
        columns = pl.ds(half * HALF, HALF)
        for core in range(2):
            pltpu.make_async_remote_copy(
                src_ref=rows_out.at[lo * 2 + core, block, :, columns],
                dst_ref=landed.at[half, block, 1 + me.core],
                send_sem=land_send, recv_sem=land_recv.at[half, block],
                device_id=me.along_y(1 if half == 0 else -1, core), device_id_type=MESH,
            ).start()

    def give_sibling(half, visit):
        block = me.block(half, *visits[visit])
        pltpu.make_async_remote_copy(
            src_ref=rows_out.at[me.lo * 2 + 1 - me.core, block, :, pl.ds(half * HALF, HALF)],
            dst_ref=landed.at[half, block, 0],
            send_sem=land_send, recv_sem=land_recv.at[half, block],
            device_id=me.sibling(), device_id_type=MESH,
        ).start()

    AHEAD = 4
    expert(lo * 2)
    for half in both:
        expert_down(lo * 2, half)
        for visit in range(AHEAD):
            give_y(half, visit)
    expert(me.lo * 2)
    for half in both:
        expert_down(me.lo * 2, half)
        for visit in range(AHEAD):
            give_sibling(half, visit)

    turn = [0, 0]

    def mixed(half, first, second):
        assert visits[turn[half]] == (first, second)
        if turn[half] + AHEAD < BLOCKS:
            give_y(half, turn[half] + AHEAD)
            give_sibling(half, turn[half] + AHEAD)
        turn[half] += 1
        block = me.block(half, first, second)
        landing(landed.at[half, block], land_recv.at[half, block])
        weight = weights[block]
        lead = weight.astype(BF16)
        trail = (weight - lead.astype(F32)).astype(BF16)
        own = rows_out[own_group, block, :, pl.ds(half * HALF, HALF)]
        parts = landed[half, block]
        rows = jnp.concatenate([own, parts[0], parts[1], parts[2]], axis=0)
        return jnp.dot(lead, rows, preferred_element_type=F32) + jnp.dot(trail, rows, preferred_element_type=F32)

    def ring(half, stage, step, src, dst, sem):
        pltpu.make_async_remote_copy(
            src_ref=src, dst_ref=dst, send_sem=ring_send, recv_sem=sem,
            device_id=me.plane(AXES[half][stage], step), device_id_type=MESH,
        ).start()

    low, high = slice(0, ROWS // 2), slice(ROWS // 2, ROWS)

    def send_far(half, stage, value, out, into, sems):
        out[...] = value.astype(BF16)
        for way, step, rows in ((0, 1, low_rows), (1, -1, high_rows)):
            ring(half, stage, step, out.at[rows], into.at[way], sems(way))

    def send_near(half, stage, way, value, far_in, far_sem, out, into, sem):
        landing(far_in, far_sem)
        passed = far_in[...].astype(F32)
        if way == 0:
            out[low] = (value[low] + passed).astype(BF16)
            out[high] = value[high].astype(BF16)
        else:
            out[low] = value[low].astype(BF16)
            out[high] = (value[high] + passed).astype(BF16)
        ring(half, stage, 1 if way == 0 else -1, out, into, sem)

    def far2(half, index):
        value = mixed(half, far_order[index], 2)
        send_far(
            half, 1, value, far2_out.at[half, index], far2_in.at[half, index],
            lambda way: far2_recv.at[half, index, way],
        )

    def near2(half, index):
        for way, second in ((0, 1), (1, -1)):
            value = mixed(half, far_order[index], second)
            send_near(
                half, 1, way, value, far2_in.at[half, index, way], far2_recv.at[half, index, way],
                near2_out.at[half, index, way], near2_in.at[half, index, way], near2_recv.at[half, index, way],
            )

    def stage1(half, index):
        value = mixed(half, far_order[index], 0)
        for way in both:
            landing(near2_in.at[half, index, way], near2_recv.at[half, index, way])
            value = value + near2_in[half, index, way].astype(F32)
        first = far_order[index]
        if first == 2:
            send_far(half, 0, value, far1_out.at[half], far1_in.at[half], lambda way: far1_recv.at[half, way])
        elif first != 0:
            way = 0 if first == 1 else 1
            send_near(
                half, 0, way, value, far1_in.at[half, way], far1_recv.at[half, way],
                near1_out.at[half, way], near1_in.at[half, way], near1_recv.at[half, way],
            )
        else:
            for way in both:
                landing(near1_in.at[half, way], near1_recv.at[half, way])
                value = value + near1_in[half, way].astype(F32)
            side_out[half] = value.astype(BF16)
            pltpu.make_async_remote_copy(
                src_ref=side_out.at[half], dst_ref=side_in.at[half],
                send_sem=side_send, recv_sem=side_recv.at[half],
                device_id=other_side, device_id_type=MESH,
            ).start()

    for half in both:
        far2(half, 0)
    for index in range(4):
        if index < 3:
            for half in both:
                far2(half, index + 1)
        for half in both:
            near2(half, index)
        if index > 0:
            for half in both:
                stage1(half, index - 1)
    for half in both:
        stage1(half, 3)
    for half in both:
        landing(side_in.at[half], side_recv.at[half])
        moe_ref[:, half * HALF : (half + 1) * HALF] = (
            side_out[half].astype(F32) + side_in[half].astype(F32)
        ).astype(BF16)

    landing(gathered.at[:, pl.ds(0, 15)], ag_send)
    landing(picked_y, pick_send)
    landing(picked_s, pick_send)
    landing(rows_out.at[pl.ds(0, 3)], land_send)
    for ref in (far2_out, near2_out, far1_out, near1_out):
        landing(ref, ring_send)
    landing(side_out, side_send)


def per_device(
    queries,
    cache_keys,
    cache_values,
    new_key,
    new_value,
    cache_lengths,
    hidden,
    norm_gain,
    expert_ids,
    router_probs,
    w_gate,
    w_up,
    w_down,
):
    vmem = pl.BlockSpec(memory_space=pltpu.VMEM)
    smem = pl.BlockSpec(memory_space=pltpu.SMEM)
    hbm = pl.BlockSpec(memory_space=pl.ANY)
    dma = pltpu.SemaphoreType.DMA

    def bf16(*shape):
        return pltpu.VMEM(shape, BF16)

    context, moe_out = pl.pallas_call(
        step_kernel,
        out_shape=(
            jax.ShapeDtypeStruct((ROWS, 32, HEAD_DIM), BF16),
            jax.ShapeDtypeStruct((ROWS, D), BF16),
        ),
        in_specs=[vmem] * 4 + [smem] + [vmem] * 3 + [hbm] * 5,
        out_specs=(vmem, vmem),
        scratch_shapes=[
            bf16(2, BLOCKS, ROWS, WIDE),
            bf16(2, BLOCKS, 2, SLOTS, HALF),
            bf16(2, BLOCKS, SLOTS, HALF),
            bf16(GROUPS, BLOCKS, SLOTS, D),
            pltpu.VMEM((BLOCKS, ROWS, GROUPS * SLOTS), F32),
            bf16(D, HIDDEN),
            bf16(D, HIDDEN),
            bf16(HIDDEN, D),
            bf16(2 * BLOCKS * SLOTS, HIDDEN),
            bf16(GROUPS, BLOCKS, SLOTS, D),
            bf16(2, BLOCKS, 3, SLOTS, HALF),
            bf16(2, 4, ROWS, HALF),
            bf16(2, 4, 2, ROWS, HALF),
            bf16(2, 4, 2, ROWS // 2, HALF),
            bf16(2, 4, 2, ROWS, HALF),
            bf16(2, ROWS, HALF),
            bf16(2, 2, ROWS, HALF),
            bf16(2, 2, ROWS // 2, HALF),
            bf16(2, 2, ROWS, HALF),
            bf16(2, ROWS, HALF),
            bf16(2, ROWS, HALF),
            bf16(2, CHUNK, KEYS, 2 * HEAD_DIM),
            bf16(2, CHUNK, KEYS, 2 * HEAD_DIM),
            dma, dma((2, 20)), dma, dma, dma((3,)), dma((2, 2)),
            dma, dma((2, BLOCKS)), dma, dma((2, 4, 2)), dma((2, 4, 2)), dma((2, 2)), dma((2, 2)), dma, dma((2,)),
        ],
        compiler_params=pltpu.CompilerParams(
            collective_id=0, has_side_effects=True, vmem_limit_bytes=58 * 1024 * 1024
        ),
        name="step",
    )(
        hidden, norm_gain.reshape(1, D), expert_ids, router_probs, cache_lengths,
        queries.reshape(ROWS, 32, HEAD_DIM), new_key, new_value,
        cache_keys, cache_values, w_gate[0], w_up[0], w_down[0],
    )
    return (context.reshape(ROWS, 32 * HEAD_DIM), moe_out)


def solution(mesh):
    in_specs = (
        P("dev", "side"),
        P("dev", None, "side"),
        P("dev", None, "side"),
        P("dev", "side"),
        P("dev", "side"),
        P("dev"),
        P("dev", None),
        P(),
        P("dev", None),
        P("dev", None),
        P("dev", None, "side"),
        P("dev", None, "side"),
        P("dev", "side", None),
    )
    out_specs = (P("dev", "side"), P("dev", None))
    return jax.shard_map(
        per_device, mesh=mesh, in_specs=in_specs, out_specs=out_specs, check_vma=False
    )
```

```python
import functools

import jax
import jax.numpy as jnp
from jax import lax
from jax.experimental import pallas as pl
from jax.experimental.pallas import tpu as pltpu
from jax.sharding import PartitionSpec as P

HEADS = 64
KV_HEADS = 4
HEAD_DIM = 128
RING = 4
BLOCKS = 16
ROWS = 32
SLOTS = 8
GROUPS = 4
D = 4096
HALF = 2048
TAIL = 128
WIDE = HALF + TAIL
MESH = pl.DeviceIdType.MESH
F32 = jnp.float32
BF16 = jnp.bfloat16


class Place:
    def __init__(self):
        self.side = lax.axis_index("side")
        dev = lax.axis_index("dev")
        self.dev = dev
        self.core = dev % 2
        self.x = (dev // 2) % RING
        self.z = (dev // 8) % RING
        self.lo = dev // 32
        self.y = self.side * 2 + self.lo

    @staticmethod
    def index(lo, z, x, core):
        return ((lo * RING + z) * RING + x) * 2 + core

    def plane(self, axis, step):
        if axis == "x":
            return (self.side, self.index(self.lo, self.z, (self.x + step) % RING, self.core))
        return (self.side, self.index(self.lo, (self.z + step) % RING, self.x, self.core))

    def along_y(self, step, core):
        y = (self.y + step) % RING
        return (y // 2, self.index(y % 2, self.z, self.x, core))

    def sibling(self):
        return (self.side, self.index(self.lo, self.z, self.x, 1 - self.core))

    def block(self, half, first, second):
        if half == 0:
            x, z = (self.x + first) % RING, (self.z + second) % RING
        else:
            z, x = (self.z + first) % RING, (self.x + second) % RING
        return z * RING + x


AXES = (("x", "z"), ("z", "x"))
NEAR = (0, -1, 1, 2)


def routing_table(ids_ref, probs_ref):
    place = lax.broadcasted_iota(jnp.int32, (TAIL, ROWS), 0)
    expert = place % 64
    ids = ids_ref[...]
    probs = probs_ref[...]
    share = probs / jnp.sum(probs, axis=0, keepdims=True)
    hit = jnp.zeros((TAIL, ROWS), F32)
    gate = jnp.zeros((TAIL, ROWS), F32)
    for k in range(ids.shape[0]):
        match = ids[k : k + 1, :] == expert
        hit = jnp.where(match, 1.0, hit)
        gate = jnp.where(match, share[k : k + 1, :], gate)
    row = lax.broadcasted_iota(jnp.int32, (ROWS, ROWS), 0)
    col = lax.broadcasted_iota(jnp.int32, (ROWS, ROWS), 1)
    before = jnp.where(row < col, 1.0, 0.0).astype(BF16)
    same = jnp.where(row == col, 1.0, 0.0).astype(BF16)
    rank = jnp.dot(hit.astype(BF16), before, preferred_element_type=F32)
    rank = jnp.where(hit > 0.5, rank, 100.0)
    lead = gate.astype(BF16).astype(F32)
    first = place < 64
    return tuple(
        lax.dot_general(
            same, jnp.where(first, rank, part).astype(BF16), (((1,), (1,)), ((), ())), preferred_element_type=F32
        ).astype(BF16)
        for part in (lead, gate - lead)
    )


CHUNK = 4
KEYS = 256
HEADS_HERE = 32
HIDDEN = 768


def step_kernel(
    hidden_ref, gain_ref, ids_ref, probs_ref, lengths_ref, queries_ref, new_key_ref, new_value_ref,
    keys_hbm, values_hbm, w_gate_hbm, w_up_hbm, w_down_hbm,
    context_ref, moe_ref,
    gathered, picked_y, picked_s, rows_in, weights, w_gate, w_up, w_down, active, rows_out,
    landed, far2_out, near2_out, far2_in, near2_in, far1_out, near1_out, far1_in, near1_in,
    side_out, side_in, keys, values, query_rows, context_rows,
    ag_send, ag_recv, pick_send, rows_recv, w_sem, kv_sem,
    land_send, land_recv, ring_send, far2_recv, near2_recv, far1_recv, near1_recv, side_send, side_recv,
):
    me = Place()
    both = range(2)
    lo = 1 - me.lo
    own_group = me.lo * 2 + me.core
    other_side = (1 - me.side, me.dev)

    w_copies = [
        pltpu.make_async_copy(w_gate_hbm, w_gate, w_sem.at[0]),
        pltpu.make_async_copy(w_up_hbm, w_up, w_sem.at[1]),
        pltpu.make_async_copy(w_down_hbm, w_down, w_sem.at[2]),
    ]

    def cache_copies(chunk):
        tokens = pl.ds(chunk * CHUNK, CHUNK)
        slot = chunk % 2
        return (
            pltpu.make_async_copy(keys_hbm.at[tokens], keys.at[slot], kv_sem.at[slot, 0]),
            pltpu.make_async_copy(values_hbm.at[tokens], values.at[slot], kv_sem.at[slot, 1]),
        )

    for chunk in range(2):
        for copy in cache_copies(chunk):
            copy.start()
    for copy in w_copies:
        copy.start()

    neighbours = (
        [me.plane(axis, step) for axis in ("x", "z") for step in (-1, 1)]
        + [me.along_y(step, core) for step in (-1, 1) for core in (0, 1)]
        + [me.sibling(), other_side]
    )
    barrier = pltpu.get_barrier_semaphore()
    for device in neighbours:
        pl.semaphore_signal(barrier, inc=1, device_id=device, device_id_type=MESH)

    wide = hidden_ref[...].astype(F32)
    inverse = lax.rsqrt(jnp.mean(wide * wide, axis=1, keepdims=True) + 1e-06)
    gain = gain_ref[...].astype(F32)
    tables = routing_table(ids_ref, probs_ref)
    own_block = me.block(0, 0, 0)
    for part in range(D // TAIL):
        half, low = divmod(part * TAIL, HALF)
        normed = wide[:, part * TAIL : (part + 1) * TAIL] * inverse * gain[part : part + 1, :]
        gathered[half, own_block, :, low : low + TAIL] = normed.astype(BF16)
    for half in both:
        gathered[half, own_block, :, HALF:WIDE] = tables[half]

    experts = (
        me.dev,
        me.index(me.lo, me.z, me.x, 1 - me.core),
        me.index(lo, me.z, me.x, 0),
        me.index(lo, me.z, me.x, 1),
    )
    slot_of = lax.broadcasted_iota(jnp.int32, (GROUPS * SLOTS, TAIL), 0)
    lane = lax.broadcasted_iota(jnp.int32, (GROUPS * SLOTS, TAIL), 1)
    wanted = jnp.zeros((GROUPS * SLOTS, TAIL), jnp.int32)
    for j in range(GROUPS):
        wanted = jnp.where(slot_of // SLOTS == j, experts[j], wanted)
    pick_rank = jnp.where(lane == wanted, 1.0, 0.0).astype(BF16)
    pick_gate = jnp.where(lane == wanted + 64, 1.0, 0.0).astype(BF16)
    pick_both = jnp.concatenate([pick_rank, pick_gate], axis=0)

    pl.semaphore_wait(barrier, len(neighbours))

    def hop(half, block, rows, stage, step, sem):
        ref = gathered.at[half, block, rows]
        return pltpu.make_async_remote_copy(
            src_ref=ref, dst_ref=ref, send_sem=ag_send, recv_sem=ag_recv.at[half, sem],
            device_id=me.plane(AXES[half][stage], step), device_id_type=MESH,
        )

    full, low_rows, high_rows = pl.ds(0, ROWS), pl.ds(0, ROWS // 2), pl.ds(ROWS // 2, ROWS // 2)

    def send_both(half, first, stage, base):
        block = me.block(half, first, 0)
        hop(half, block, full, stage, 1, base).start()
        hop(half, block, full, stage, -1, base + 1).start()

    def landing(ref, sem):
        pltpu.make_async_copy(ref, ref, sem).wait()

    def take_full(half, first, stage, base):
        for step, rows, sem in ((-1, low_rows, base), (1, high_rows, base + 1)):
            block = me.block(half, step, 0) if stage == 0 else me.block(half, first, step)
            landing(gathered.at[half, block], ag_recv.at[half, sem])
            hop(half, block, rows, stage, -step, sem + 2).start()

    def take_far(half, first, stage, base):
        block = me.block(half, 2, 0) if stage == 0 else me.block(half, first, 2)
        landing(gathered.at[half, block, low_rows], ag_recv.at[half, base + 2])
        landing(gathered.at[half, block, high_rows], ag_recv.at[half, base + 3])

    def select(half, first, second):
        block = me.block(half, first, second)
        table = gathered[half, block, :, HALF:WIDE]
        rank = lax.dot_general(pick_rank, table, (((1,), (1,)), ((), ())), preferred_element_type=F32)
        slot = (lax.broadcasted_iota(jnp.int32, (GROUPS * SLOTS, ROWS), 0) % SLOTS).astype(F32)
        hot = jnp.where(rank == slot, 1.0, 0.0).astype(BF16)
        both_ways = lax.dot_general(table, pick_both, (((1,), (1,)), ((), ())), preferred_element_type=F32)
        slot = (lax.broadcasted_iota(jnp.int32, (ROWS, GROUPS * SLOTS), 1) % SLOTS).astype(F32)
        weights[half, block] = jnp.where(
            both_ways[:, 0 : GROUPS * SLOTS] == slot, both_ways[:, GROUPS * SLOTS :], 0.0
        ).astype(BF16)
        chosen = jnp.dot(hot, gathered[half, block, :, 0:HALF], preferred_element_type=F32).astype(BF16)
        columns = pl.ds(half * HALF, HALF)
        for core in range(2):
            picked_y[half, block, core] = chosen[16 + 8 * core : 24 + 8 * core]
            pltpu.make_async_remote_copy(
                src_ref=picked_y.at[half, block, core],
                dst_ref=rows_in.at[own_group, block, :, columns],
                send_sem=pick_send, recv_sem=rows_recv,
                device_id=me.along_y(1 if half == 0 else -1, core), device_id_type=MESH,
            ).start()
        picked_s[half, block] = chosen[8:16]
        pltpu.make_async_remote_copy(
            src_ref=picked_s.at[half, block],
            dst_ref=rows_in.at[own_group, block, :, columns],
            send_sem=pick_send, recv_sem=rows_recv,
            device_id=me.sibling(), device_id_type=MESH,
        ).start()
        rows_in[own_group, block, :, columns] = chosen[0:8]

    def attend(chunk):
        slot = chunk % 2
        for copy in cache_copies(chunk):
            copy.wait()
        scale = HEAD_DIM ** (-0.5)
        position = lax.broadcasted_iota(jnp.int32, (HEADS_HERE, KEYS), 1)
        upper = lax.broadcasted_iota(jnp.int32, (HEADS_HERE, HEAD_DIM), 0) < HEADS_HERE // 2

        def by_group(row):
            return jnp.where(upper, row[:, 0:HEAD_DIM], row[:, HEAD_DIM:])

        for item in range(CHUNK):
            token = chunk * CHUNK + item
            heads = slice(token * HEADS_HERE, (token + 1) * HEADS_HERE)
            query = query_rows[heads]
            split = jnp.concatenate([jnp.where(upper, query, 0.0), jnp.where(upper, 0.0, query)], axis=1)
            scores = lax.dot_general(
                split.astype(BF16), keys[slot, item], (((1,), (1,)), ((), ())), preferred_element_type=F32
            )
            scores = jnp.where(position < lengths_ref[token], scores * scale, -1e30)
            own_key = by_group(new_key_ref[token : token + 1, :].astype(F32))
            own = jnp.sum(query * own_key, axis=1, keepdims=True) * scale
            top = jnp.maximum(jnp.max(scores, axis=1, keepdims=True), own)
            scores = jnp.exp(scores - top)
            own = jnp.exp(own - top)
            share = 1.0 / (jnp.sum(scores, axis=1, keepdims=True) + own)
            probs = (scores * share).astype(BF16)
            own = (own * share).astype(BF16).astype(F32)
            mixed = by_group(jnp.dot(probs, values[slot, item], preferred_element_type=F32))
            context_rows[heads] = mixed + own * by_group(new_value_ref[token : token + 1, :].astype(F32))
        if chunk + 2 < ROWS // CHUNK:
            for copy in cache_copies(chunk + 2):
                copy.start()

    for half in both:
        send_both(half, 0, 0, 0)
    for half in both:
        send_both(half, 0, 1, 4)
    for half in both:
        select(half, 0, 0)
    for head in range(HEADS_HERE):
        lanes = slice(head * HEAD_DIM, (head + 1) * HEAD_DIM)
        query_rows[pl.ds(head, ROWS, stride=HEADS_HERE), :] = queries_ref[:, lanes].astype(F32)
    attend(0)
    for half in both:
        take_full(half, 0, 0, 0)
        send_both(half, -1, 1, 8)
    for half in both:
        select(half, -1, 0)
        select(half, 1, 0)
    attend(1)
    for half in both:
        take_full(half, 0, 1, 4)
        send_both(half, 1, 1, 12)
    for half in both:
        take_far(half, 0, 0, 0)
    for half in both:
        select(half, 2, 0)
        select(half, 0, -1)
        select(half, 0, 1)
    attend(2)
    for index in range(1, 4):
        first = NEAR[index]
        for half in both:
            take_full(half, first, 1, 4 + 4 * index)
            if index == 1:
                send_both(half, 2, 1, 16)
        for half in both:
            take_far(half, NEAR[index - 1], 1, 4 * index)
        for half in both:
            select(half, first, -1)
            select(half, first, 1)
            select(half, NEAR[index - 1], 2)
        attend(2 + index)
    for half in both:
        take_far(half, 2, 1, 16)
        select(half, 2, 2)
    attend(6)

    attend(7)

    for head in range(HEADS_HERE):
        lanes = slice(head * HEAD_DIM, (head + 1) * HEAD_DIM)
        context_ref[:, lanes] = context_rows[pl.ds(head, ROWS, stride=HEADS_HERE), :].astype(BF16)

    for copy in w_copies:
        copy.wait()
    landing(rows_in.at[pl.ds(0, 3)], rows_recv)

    def expert(base):
        rows = rows_in[pl.ds(base, 2)].reshape(2 * BLOCKS * SLOTS, D)
        for low in range(0, HIDDEN, 256):
            columns = slice(low, low + 256)
            gate = jnp.dot(rows, w_gate[:, columns], preferred_element_type=F32)
            up = jnp.dot(rows, w_up[:, columns], preferred_element_type=F32)
            active[:, columns] = (gate / (1.0 + jnp.exp(-gate)) * up).astype(BF16)

    def expert_down(base, half):
        for low in range(half * HALF, (half + 1) * HALF, 512):
            columns = slice(low, low + 512)
            out = jnp.dot(active[...], w_down[:, columns], preferred_element_type=F32).astype(BF16)
            rows_out[pl.ds(base, 2), :, :, columns] = out.reshape(2, BLOCKS, SLOTS, 512)

    far_order = (2, 1, -1, 0)
    visits = (
        (2, 2), (1, 2), (2, 1), (2, -1), (-1, 2), (1, 1), (1, -1), (2, 0),
        (0, 2), (-1, 1), (-1, -1), (1, 0), (0, 1), (0, -1), (-1, 0), (0, 0),
    )

    def give_y(half, visit):
        block = me.block(half, *visits[visit])
        columns = pl.ds(half * HALF, HALF)
        for core in range(2):
            pltpu.make_async_remote_copy(
                src_ref=rows_out.at[lo * 2 + core, block, :, columns],
                dst_ref=landed.at[half, block, 1 + me.core],
                send_sem=land_send, recv_sem=land_recv.at[half, block],
                device_id=me.along_y(1 if half == 0 else -1, core), device_id_type=MESH,
            ).start()

    def give_sibling(half, visit):
        block = me.block(half, *visits[visit])
        pltpu.make_async_remote_copy(
            src_ref=rows_out.at[me.lo * 2 + 1 - me.core, block, :, pl.ds(half * HALF, HALF)],
            dst_ref=landed.at[half, block, 0],
            send_sem=land_send, recv_sem=land_recv.at[half, block],
            device_id=me.sibling(), device_id_type=MESH,
        ).start()

    AHEAD = 6
    expert(lo * 2)
    for half in both:
        expert_down(lo * 2, half)
        for visit in range(AHEAD):
            give_y(half, visit)
    expert(me.lo * 2)
    for half in both:
        expert_down(me.lo * 2, half)
        for visit in range(AHEAD):
            give_sibling(half, visit)

    turn = [0, 0]

    def mixed(half, first, second):
        assert visits[turn[half]] == (first, second)
        if turn[half] + AHEAD < BLOCKS:
            give_y(half, turn[half] + AHEAD)
            give_sibling(half, turn[half] + AHEAD)
        turn[half] += 1
        block = me.block(half, first, second)
        landing(landed.at[half, block], land_recv.at[half, block])
        own = rows_out[own_group, block, :, pl.ds(half * HALF, HALF)]
        parts = landed[half, block]
        rows = jnp.concatenate([own, parts[0], parts[1], parts[2]], axis=0)
        return jnp.dot(weights[0, block], rows, preferred_element_type=F32) + jnp.dot(
            weights[1, block], rows, preferred_element_type=F32
        )

    def ring(half, stage, step, src, dst, sem):
        pltpu.make_async_remote_copy(
            src_ref=src, dst_ref=dst, send_sem=ring_send, recv_sem=sem,
            device_id=me.plane(AXES[half][stage], step), device_id_type=MESH,
        ).start()

    low, high = slice(0, ROWS // 2), slice(ROWS // 2, ROWS)

    def send_far(half, stage, value, out, into, sems):
        out[...] = value.astype(BF16)
        for way, step, rows in ((0, 1, low_rows), (1, -1, high_rows)):
            ring(half, stage, step, out.at[rows], into.at[way], sems(way))

    def send_near(half, stage, way, value, far_in, far_sem, out, into, sem):
        landing(far_in, far_sem)
        passed = far_in[...].astype(F32)
        if way == 0:
            out[low] = (value[low] + passed).astype(BF16)
            out[high] = value[high].astype(BF16)
        else:
            out[low] = value[low].astype(BF16)
            out[high] = (value[high] + passed).astype(BF16)
        ring(half, stage, 1 if way == 0 else -1, out, into, sem)

    def far2(half, index):
        value = mixed(half, far_order[index], 2)
        send_far(
            half, 1, value, far2_out.at[half, index], far2_in.at[half, index],
            lambda way: far2_recv.at[half, index, way],
        )

    def near2(half, index):
        for way, second in ((0, 1), (1, -1)):
            value = mixed(half, far_order[index], second)
            send_near(
                half, 1, way, value, far2_in.at[half, index, way], far2_recv.at[half, index, way],
                near2_out.at[half, index, way], near2_in.at[half, index, way], near2_recv.at[half, index, way],
            )

    def stage1(half, index):
        value = mixed(half, far_order[index], 0)
        for way in both:
            landing(near2_in.at[half, index, way], near2_recv.at[half, index, way])
            value = value + near2_in[half, index, way].astype(F32)
        first = far_order[index]
        if first == 2:
            send_far(half, 0, value, far1_out.at[half], far1_in.at[half], lambda way: far1_recv.at[half, way])
        elif first != 0:
            way = 0 if first == 1 else 1
            send_near(
                half, 0, way, value, far1_in.at[half, way], far1_recv.at[half, way],
                near1_out.at[half, way], near1_in.at[half, way], near1_recv.at[half, way],
            )
        else:
            for way in both:
                landing(near1_in.at[half, way], near1_recv.at[half, way])
                value = value + near1_in[half, way].astype(F32)
            side_out[half] = value.astype(BF16)
            pltpu.make_async_remote_copy(
                src_ref=side_out.at[half], dst_ref=side_in.at[half],
                send_sem=side_send, recv_sem=side_recv.at[half],
                device_id=other_side, device_id_type=MESH,
            ).start()

    for half in both:
        far2(half, 0)
    for index in range(4):
        if index < 3:
            for half in both:
                far2(half, index + 1)
        for half in both:
            near2(half, index)
        if index > 0:
            for half in both:
                stage1(half, index - 1)
    for half in both:
        stage1(half, 3)
    for half in both:
        landing(side_in.at[half], side_recv.at[half])
        moe_ref[:, half * HALF : (half + 1) * HALF] = (
            side_out[half].astype(F32) + side_in[half].astype(F32)
        ).astype(BF16)

    landing(gathered.at[:, pl.ds(0, 15)], ag_send)
    landing(picked_y, pick_send)
    landing(picked_s, pick_send)
    landing(rows_out.at[pl.ds(0, 3)], land_send)
    for ref in (far2_out, near2_out, far1_out, near1_out):
        landing(ref, ring_send)
    landing(side_out, side_send)


def per_device(
    queries,
    cache_keys,
    cache_values,
    new_key,
    new_value,
    cache_lengths,
    hidden,
    norm_gain,
    expert_ids,
    router_probs,
    w_gate,
    w_up,
    w_down,
):
    vmem = pl.BlockSpec(memory_space=pltpu.VMEM)
    smem = pl.BlockSpec(memory_space=pltpu.SMEM)
    hbm = pl.BlockSpec(memory_space=pl.ANY)
    dma = pltpu.SemaphoreType.DMA

    def bf16(*shape):
        return pltpu.VMEM(shape, BF16)

    context, moe_out = pl.pallas_call(
        step_kernel,
        out_shape=(
            jax.ShapeDtypeStruct((ROWS, HEADS_HERE * HEAD_DIM), BF16),
            jax.ShapeDtypeStruct((ROWS, D), BF16),
        ),
        in_specs=[vmem] * 4 + [smem] + [vmem] * 3 + [hbm] * 5,
        out_specs=(vmem, vmem),
        scratch_shapes=[
            bf16(2, BLOCKS, ROWS, WIDE),
            bf16(2, BLOCKS, 2, SLOTS, HALF),
            bf16(2, BLOCKS, SLOTS, HALF),
            bf16(GROUPS, BLOCKS, SLOTS, D),
            bf16(2, BLOCKS, ROWS, GROUPS * SLOTS),
            bf16(D, HIDDEN),
            bf16(D, HIDDEN),
            bf16(HIDDEN, D),
            bf16(2 * BLOCKS * SLOTS, HIDDEN),
            bf16(GROUPS, BLOCKS, SLOTS, D),
            bf16(2, BLOCKS, 3, SLOTS, HALF),
            bf16(2, 4, ROWS, HALF),
            bf16(2, 4, 2, ROWS, HALF),
            bf16(2, 4, 2, ROWS // 2, HALF),
            bf16(2, 4, 2, ROWS, HALF),
            bf16(2, ROWS, HALF),
            bf16(2, 2, ROWS, HALF),
            bf16(2, 2, ROWS // 2, HALF),
            bf16(2, 2, ROWS, HALF),
            bf16(2, ROWS, HALF),
            bf16(2, ROWS, HALF),
            bf16(2, CHUNK, KEYS, 2 * HEAD_DIM),
            bf16(2, CHUNK, KEYS, 2 * HEAD_DIM),
            pltpu.VMEM((ROWS * HEADS_HERE, HEAD_DIM), F32),
            pltpu.VMEM((ROWS * HEADS_HERE, HEAD_DIM), F32),
            dma, dma((2, 20)), dma, dma, dma((3,)), dma((2, 2)),
            dma, dma((2, BLOCKS)), dma, dma((2, 4, 2)), dma((2, 4, 2)), dma((2, 2)), dma((2, 2)), dma, dma((2,)),
        ],
        compiler_params=pltpu.CompilerParams(
            collective_id=0, has_side_effects=True, vmem_limit_bytes=58 * 1024 * 1024
        ),
        name="step",
    )(
        hidden, norm_gain.reshape(D // TAIL, TAIL), expert_ids.T, router_probs.T, cache_lengths,
        queries, new_key, new_value,
        cache_keys, cache_values, w_gate[0], w_up[0], w_down[0],
    )
    return (context, moe_out)


def solution(mesh):
    in_specs = (
        P("dev", "side"),
        P("dev", None, "side"),
        P("dev", None, "side"),
        P("dev", "side"),
        P("dev", "side"),
        P("dev"),
        P("dev", None),
        P(),
        P("dev", None),
        P("dev", None),
        P("dev", None, "side"),
        P("dev", None, "side"),
        P("dev", "side", None),
    )
    out_specs = (P("dev", "side"), P("dev", None))
    return jax.shard_map(
        per_device, mesh=mesh, in_specs=in_specs, out_specs=out_specs, check_vma=False
    )
```

```python
import functools

import jax
import jax.numpy as jnp
from jax import lax
from jax.experimental import pallas as pl
from jax.experimental.pallas import tpu as pltpu
from jax.sharding import PartitionSpec as P

HEADS = 64
KV_HEADS = 4
HEAD_DIM = 128
RING = 4
BLOCKS = 16
ROWS = 32
SLOTS = 8
GROUPS = 4
D = 4096
HALF = 2048
TAIL = 128
WIDE = HALF + TAIL
MESH = pl.DeviceIdType.MESH
F32 = jnp.float32
BF16 = jnp.bfloat16


class Place:
    def __init__(self):
        self.side = lax.axis_index("side")
        dev = lax.axis_index("dev")
        self.dev = dev
        self.core = dev % 2
        self.x = (dev // 2) % RING
        self.z = (dev // 8) % RING
        self.lo = dev // 32
        self.y = self.side * 2 + self.lo

    @staticmethod
    def index(lo, z, x, core):
        return ((lo * RING + z) * RING + x) * 2 + core

    def plane(self, axis, step):
        if axis == "x":
            return (self.side, self.index(self.lo, self.z, (self.x + step) % RING, self.core))
        return (self.side, self.index(self.lo, (self.z + step) % RING, self.x, self.core))

    def along_y(self, step, core):
        y = (self.y + step) % RING
        return (y // 2, self.index(y % 2, self.z, self.x, core))

    def sibling(self):
        return (self.side, self.index(self.lo, self.z, self.x, 1 - self.core))

    def block(self, half, first, second):
        if half == 0:
            x, z = (self.x + first) % RING, (self.z + second) % RING
        else:
            z, x = (self.z + first) % RING, (self.x + second) % RING
        return z * RING + x


AXES = (("x", "z"), ("z", "x"))
NEAR = (0, -1, 1, 2)
LISTED = (
    (2, 2), (1, 2), (2, 1), (-1, 2), (2, -1), (1, 1), (0, 2), (2, 0),
    (1, -1), (-1, 1), (-1, -1), (0, 1), (1, 0), (0, -1), (-1, 0), (0, 0),
)


def listed(half, first, second):
    return LISTED.index((first, second) if half == 0 else (second, first))


def routing_table(ids_ref, probs_ref):
    place = lax.broadcasted_iota(jnp.int32, (TAIL, ROWS), 0)
    expert = place % 64
    ids = ids_ref[...]
    probs = probs_ref[...]
    share = probs / jnp.sum(probs, axis=0, keepdims=True)
    hit = jnp.zeros((TAIL, ROWS), F32)
    gate = jnp.zeros((TAIL, ROWS), F32)
    for k in range(ids.shape[0]):
        match = ids[k : k + 1, :] == expert
        hit = jnp.where(match, 1.0, hit)
        gate = jnp.where(match, share[k : k + 1, :], gate)
    row = lax.broadcasted_iota(jnp.int32, (ROWS, ROWS), 0)
    col = lax.broadcasted_iota(jnp.int32, (ROWS, ROWS), 1)
    before = jnp.where(row < col, 1.0, 0.0).astype(BF16)
    same = jnp.where(row == col, 1.0, 0.0).astype(BF16)
    rank = jnp.dot(hit.astype(BF16), before, preferred_element_type=F32)
    rank = jnp.where(hit > 0.5, rank, 100.0)
    lead = gate.astype(BF16).astype(F32)
    first = place < 64
    return tuple(
        lax.dot_general(
            same, jnp.where(first, rank, part).astype(BF16), (((1,), (1,)), ((), ())), preferred_element_type=F32
        ).astype(BF16)
        for part in (lead, gate - lead)
    )


CHUNK = 4
KEYS = 256
HEADS_HERE = 32
HIDDEN = 768


def step_kernel(
    hidden_ref, gain_ref, ids_ref, probs_ref, lengths_ref, queries_ref, new_key_ref, new_value_ref,
    keys_hbm, values_hbm, w_gate_hbm, w_up_hbm, w_down_hbm,
    context_ref, moe_ref,
    gathered, picked_y, picked_s, rows_in, weights, w_gate, w_up, w_down, active, rows_out,
    landed, far2_out, near2_out, far2_in, near2_in, far1_out, near1_out, far1_in, near1_in,
    side_out, side_in, keys, values, query_rows, context_rows,
    ag_send, ag_recv, pick_send, rows_recv, w_sem, kv_sem,
    land_send, land_recv, ring_send, far2_recv, near2_recv, far1_recv, near1_recv, side_send, side_recv,
):
    me = Place()
    both = range(2)
    lo = 1 - me.lo
    own_group = me.lo * 2 + me.core
    other_side = (1 - me.side, me.dev)

    w_copies = [
        pltpu.make_async_copy(w_gate_hbm, w_gate, w_sem.at[0]),
        pltpu.make_async_copy(w_up_hbm, w_up, w_sem.at[1]),
        pltpu.make_async_copy(w_down_hbm, w_down, w_sem.at[2]),
    ]

    def cache_copies(chunk):
        tokens = pl.ds(chunk * CHUNK, CHUNK)
        slot = chunk % 2
        return (
            pltpu.make_async_copy(keys_hbm.at[tokens], keys.at[slot], kv_sem.at[slot, 0]),
            pltpu.make_async_copy(values_hbm.at[tokens], values.at[slot], kv_sem.at[slot, 1]),
        )

    for chunk in range(2):
        for copy in cache_copies(chunk):
            copy.start()
    for copy in w_copies:
        copy.start()

    neighbours = (
        [me.plane(axis, step) for axis in ("x", "z") for step in (-1, 1)]
        + [me.along_y(step, core) for step in (-1, 1) for core in (0, 1)]
        + [me.sibling(), other_side]
    )
    barrier = pltpu.get_barrier_semaphore()
    for device in neighbours:
        pl.semaphore_signal(barrier, inc=1, device_id=device, device_id_type=MESH)

    wide = hidden_ref[...].astype(F32)
    inverse = lax.rsqrt(jnp.mean(wide * wide, axis=1, keepdims=True) + 1e-06)
    gain = gain_ref[...].astype(F32)
    tables = routing_table(ids_ref, probs_ref)
    own_block = me.block(0, 0, 0)
    for part in range(D // TAIL):
        half, low = divmod(part * TAIL, HALF)
        normed = wide[:, part * TAIL : (part + 1) * TAIL] * inverse * gain[part : part + 1, :]
        gathered[half, own_block, :, low : low + TAIL] = normed.astype(BF16)
    for half in both:
        gathered[half, own_block, :, HALF:WIDE] = tables[half]

    experts = (
        me.dev,
        me.index(me.lo, me.z, me.x, 1 - me.core),
        me.index(lo, me.z, me.x, 0),
        me.index(lo, me.z, me.x, 1),
    )
    slot_of = lax.broadcasted_iota(jnp.int32, (GROUPS * SLOTS, TAIL), 0)
    lane = lax.broadcasted_iota(jnp.int32, (GROUPS * SLOTS, TAIL), 1)
    wanted = jnp.zeros((GROUPS * SLOTS, TAIL), jnp.int32)
    for j in range(GROUPS):
        wanted = jnp.where(slot_of // SLOTS == j, experts[j], wanted)
    pick_rank = jnp.where(lane == wanted, 1.0, 0.0).astype(BF16)
    pick_gate = jnp.where(lane == wanted + 64, 1.0, 0.0).astype(BF16)
    pick_both = jnp.concatenate([pick_rank, pick_gate], axis=0)

    pl.semaphore_wait(barrier, len(neighbours))

    def hop(half, block, rows, stage, step, sem):
        ref = gathered.at[half, block, rows]
        return pltpu.make_async_remote_copy(
            src_ref=ref, dst_ref=ref, send_sem=ag_send, recv_sem=ag_recv.at[half, sem],
            device_id=me.plane(AXES[half][stage], step), device_id_type=MESH,
        )

    full, low_rows, high_rows = pl.ds(0, ROWS), pl.ds(0, ROWS // 2), pl.ds(ROWS // 2, ROWS // 2)

    def send_both(half, first, stage, base):
        block = me.block(half, first, 0)
        hop(half, block, full, stage, 1, base).start()
        hop(half, block, full, stage, -1, base + 1).start()

    def landing(ref, sem):
        pltpu.make_async_copy(ref, ref, sem).wait()

    def take_full(half, first, stage, base):
        for step, rows, sem in ((-1, low_rows, base), (1, high_rows, base + 1)):
            block = me.block(half, step, 0) if stage == 0 else me.block(half, first, step)
            landing(gathered.at[half, block], ag_recv.at[half, sem])
            hop(half, block, rows, stage, -step, sem + 2).start()

    def take_far(half, first, stage, base):
        block = me.block(half, 2, 0) if stage == 0 else me.block(half, first, 2)
        landing(gathered.at[half, block, low_rows], ag_recv.at[half, base + 2])
        landing(gathered.at[half, block, high_rows], ag_recv.at[half, base + 3])

    def select(half, first, second):
        block = me.block(half, first, second)
        table = gathered[half, block, :, HALF:WIDE]
        rank = lax.dot_general(pick_rank, table, (((1,), (1,)), ((), ())), preferred_element_type=F32)
        slot = (lax.broadcasted_iota(jnp.int32, (GROUPS * SLOTS, ROWS), 0) % SLOTS).astype(F32)
        hot = jnp.where(rank == slot, 1.0, 0.0).astype(BF16)
        both_ways = lax.dot_general(table, pick_both, (((1,), (1,)), ((), ())), preferred_element_type=F32)
        slot = (lax.broadcasted_iota(jnp.int32, (ROWS, GROUPS * SLOTS), 1) % SLOTS).astype(F32)
        weights[half, listed(half, first, second)] = jnp.where(
            both_ways[:, 0 : GROUPS * SLOTS] == slot, both_ways[:, GROUPS * SLOTS :], 0.0
        ).astype(BF16)
        chosen = jnp.dot(hot, gathered[half, block, :, 0:HALF], preferred_element_type=F32).astype(BF16)
        columns = pl.ds(half * HALF, HALF)
        place = listed(half, first, second)
        for core in range(2):
            picked_y[half, block, core] = chosen[16 + 8 * core : 24 + 8 * core]
            pltpu.make_async_remote_copy(
                src_ref=picked_y.at[half, block, core],
                dst_ref=rows_in.at[own_group, place, :, columns],
                send_sem=pick_send, recv_sem=rows_recv.at[1],
                device_id=me.along_y(1 if half == 0 else -1, core), device_id_type=MESH,
            ).start()
        picked_s[half, block] = chosen[8:16]
        pltpu.make_async_remote_copy(
            src_ref=picked_s.at[half, block],
            dst_ref=rows_in.at[own_group, place, :, columns],
            send_sem=pick_send, recv_sem=rows_recv.at[0],
            device_id=me.sibling(), device_id_type=MESH,
        ).start()
        rows_in[own_group, place, :, columns] = chosen[0:8]

    def attend(chunk):
        slot = chunk % 2
        for copy in cache_copies(chunk):
            copy.wait()
        scale = HEAD_DIM ** (-0.5)
        position = lax.broadcasted_iota(jnp.int32, (HEADS_HERE, KEYS), 1)
        upper = lax.broadcasted_iota(jnp.int32, (HEADS_HERE, HEAD_DIM), 0) < HEADS_HERE // 2

        def by_group(row):
            return jnp.where(upper, row[:, 0:HEAD_DIM], row[:, HEAD_DIM:])

        for item in range(CHUNK):
            token = chunk * CHUNK + item
            heads = slice(token * HEADS_HERE, (token + 1) * HEADS_HERE)
            query = query_rows[heads]
            split = jnp.concatenate([jnp.where(upper, query, 0.0), jnp.where(upper, 0.0, query)], axis=1)
            scores = lax.dot_general(
                split.astype(BF16), keys[slot, item], (((1,), (1,)), ((), ())), preferred_element_type=F32
            )
            scores = jnp.where(position < lengths_ref[token], scores * scale, -1e30)
            own_key = by_group(new_key_ref[token : token + 1, :].astype(F32))
            own = jnp.sum(query * own_key, axis=1, keepdims=True) * scale
            top = jnp.maximum(jnp.max(scores, axis=1, keepdims=True), own)
            scores = jnp.exp(scores - top)
            own = jnp.exp(own - top)
            share = 1.0 / (jnp.sum(scores, axis=1, keepdims=True) + own)
            probs = (scores * share).astype(BF16)
            own = (own * share).astype(BF16).astype(F32)
            mixed = by_group(jnp.dot(probs, values[slot, item], preferred_element_type=F32))
            context_rows[heads] = mixed + own * by_group(new_value_ref[token : token + 1, :].astype(F32))
        if chunk + 2 < ROWS // CHUNK:
            for copy in cache_copies(chunk + 2):
                copy.start()

    for half in both:
        send_both(half, 0, 0, 0)
    for half in both:
        send_both(half, 0, 1, 4)
    for half in both:
        select(half, 0, 0)
    for head in range(HEADS_HERE):
        lanes = slice(head * HEAD_DIM, (head + 1) * HEAD_DIM)
        query_rows[pl.ds(head, ROWS, stride=HEADS_HERE), :] = queries_ref[:, lanes].astype(F32)
    attend(0)
    for half in both:
        take_full(half, 0, 0, 0)
        send_both(half, -1, 1, 8)
    for half in both:
        select(half, -1, 0)
        select(half, 1, 0)
    attend(1)
    for half in both:
        take_full(half, 0, 1, 4)
        send_both(half, 1, 1, 12)
    for half in both:
        take_far(half, 0, 0, 0)
    for half in both:
        select(half, 2, 0)
        select(half, 0, -1)
        select(half, 0, 1)
    attend(2)
    for index in range(1, 4):
        first = NEAR[index]
        for half in both:
            take_full(half, first, 1, 4 + 4 * index)
            if index == 1:
                send_both(half, 2, 1, 16)
        for half in both:
            take_far(half, NEAR[index - 1], 1, 4 * index)
        for half in both:
            select(half, first, -1)
            select(half, first, 1)
            select(half, NEAR[index - 1], 2)
        attend(2 + index)
    for half in both:
        take_far(half, 2, 1, 16)
        select(half, 2, 2)
    PART = BLOCKS // 2

    def expert(base, part):
        rows = rows_in[pl.ds(base, 2), part * PART : (part + 1) * PART].reshape(2 * PART * SLOTS, D)
        for low in range(0, HIDDEN, 256):
            columns = slice(low, low + 256)
            gate = jnp.dot(rows, w_gate[:, columns], preferred_element_type=F32)
            up = jnp.dot(rows, w_up[:, columns], preferred_element_type=F32)
            active[:, columns] = (gate / (1.0 + jnp.exp(-gate)) * up).astype(BF16)

    def expert_down(base, part, half):
        for low in range(half * HALF, (half + 1) * HALF, 512):
            columns = slice(low, low + 512)
            out = jnp.dot(active[...], w_down[:, columns], preferred_element_type=F32).astype(BF16)
            rows_out[pl.ds(base, 2), part * PART : (part + 1) * PART, :, columns] = out.reshape(2, PART, SLOTS, 512)

    far_order = (2, 1, -1, 0)
    visits = (
        (2, 2), (1, 2), (2, 1), (2, -1), (-1, 2), (1, 1), (1, -1), (2, 0),
        (0, 2), (-1, 1), (-1, -1), (1, 0), (0, 1), (0, -1), (-1, 0), (0, 0),
    )

    def give_y(half, visit):
        place = listed(half, *visits[visit])
        columns = pl.ds(half * HALF, HALF)
        for core in range(2):
            pltpu.make_async_remote_copy(
                src_ref=rows_out.at[lo * 2 + core, place, :, columns],
                dst_ref=landed.at[half, visit, 1 + me.core],
                send_sem=land_send, recv_sem=land_recv.at[half, visit],
                device_id=me.along_y(1 if half == 0 else -1, core), device_id_type=MESH,
            ).start()

    def give_sibling(half, visit):
        place = listed(half, *visits[visit])
        pltpu.make_async_remote_copy(
            src_ref=rows_out.at[me.lo * 2 + 1 - me.core, place, :, pl.ds(half * HALF, HALF)],
            dst_ref=landed.at[half, visit, 0],
            send_sem=land_send, recv_sem=land_recv.at[half, visit],
            device_id=me.sibling(), device_id_type=MESH,
        ).start()

    AHEAD = 6
    for copy in w_copies:
        copy.wait()
    landing(rows_in.at[0], rows_recv.at[0])
    expert(me.lo * 2, 0)
    for half in both:
        expert_down(me.lo * 2, 0, half)
    landing(rows_in.at[pl.ds(0, 2)], rows_recv.at[1])
    expert(lo * 2, 0)
    for half in both:
        expert_down(lo * 2, 0, half)
        for visit in range(AHEAD):
            give_y(half, visit)
            give_sibling(half, visit)
    for base in (lo * 2, me.lo * 2):
        expert(base, 1)
        for half in both:
            expert_down(base, 1, half)

    turn = [0, 0]

    def mixed(half, first, second):
        assert visits[turn[half]] == (first, second)
        if turn[half] + AHEAD < BLOCKS:
            give_y(half, turn[half] + AHEAD)
            give_sibling(half, turn[half] + AHEAD)
        visit = turn[half]
        turn[half] += 1
        place = listed(half, first, second)
        landing(landed.at[half, visit], land_recv.at[half, visit])
        own = rows_out[own_group, place, :, half * HALF : (half + 1) * HALF]
        parts = landed[half, visit]
        rows = jnp.concatenate([own, parts[0], parts[1], parts[2]], axis=0)
        return jnp.dot(weights[0, place], rows, preferred_element_type=F32) + jnp.dot(
            weights[1, place], rows, preferred_element_type=F32
        )

    def ring(half, stage, step, src, dst, sem):
        pltpu.make_async_remote_copy(
            src_ref=src, dst_ref=dst, send_sem=ring_send, recv_sem=sem,
            device_id=me.plane(AXES[half][stage], step), device_id_type=MESH,
        ).start()

    low, high = slice(0, ROWS // 2), slice(ROWS // 2, ROWS)

    def send_far(half, stage, value, out, into, sems):
        out[...] = value.astype(BF16)
        for way, step, rows in ((0, 1, low_rows), (1, -1, high_rows)):
            ring(half, stage, step, out.at[rows], into.at[way], sems(way))

    def send_near(half, stage, way, value, far_in, far_sem, out, into, sem):
        landing(far_in, far_sem)
        passed = far_in[...].astype(F32)
        if way == 0:
            out[low] = (value[low] + passed).astype(BF16)
            out[high] = value[high].astype(BF16)
        else:
            out[low] = value[low].astype(BF16)
            out[high] = (value[high] + passed).astype(BF16)
        ring(half, stage, 1 if way == 0 else -1, out, into, sem)

    def far2(half, index):
        value = mixed(half, far_order[index], 2)
        send_far(
            half, 1, value, far2_out.at[half, index], far2_in.at[half, index],
            lambda way: far2_recv.at[half, index, way],
        )

    def near2(half, index):
        for way, second in ((0, 1), (1, -1)):
            value = mixed(half, far_order[index], second)
            send_near(
                half, 1, way, value, far2_in.at[half, index, way], far2_recv.at[half, index, way],
                near2_out.at[half, index, way], near2_in.at[half, index, way], near2_recv.at[half, index, way],
            )

    def stage1(half, index):
        value = mixed(half, far_order[index], 0)
        for way in both:
            landing(near2_in.at[half, index, way], near2_recv.at[half, index, way])
            value = value + near2_in[half, index, way].astype(F32)
        first = far_order[index]
        if first == 2:
            send_far(half, 0, value, far1_out.at[half], far1_in.at[half], lambda way: far1_recv.at[half, way])
        elif first != 0:
            way = 0 if first == 1 else 1
            send_near(
                half, 0, way, value, far1_in.at[half, way], far1_recv.at[half, way],
                near1_out.at[half, way], near1_in.at[half, way], near1_recv.at[half, way],
            )
        else:
            for way in both:
                landing(near1_in.at[half, way], near1_recv.at[half, way])
                value = value + near1_in[half, way].astype(F32)
            side_out[half] = value.astype(BF16)
            pltpu.make_async_remote_copy(
                src_ref=side_out.at[half], dst_ref=side_in.at[half],
                send_sem=side_send, recv_sem=side_recv.at[half],
                device_id=other_side, device_id_type=MESH,
            ).start()

    for half in both:
        far2(half, 0)
    for index in range(4):
        if index < 3:
            for half in both:
                far2(half, index + 1)
        for half in both:
            near2(half, index)
        if index > 0:
            for half in both:
                stage1(half, index - 1)
        if index == 1:
            attend(6)
        elif index == 2:
            attend(7)
    for head in range(HEADS_HERE):
        lanes = slice(head * HEAD_DIM, (head + 1) * HEAD_DIM)
        context_ref[:, lanes] = context_rows[pl.ds(head, ROWS, stride=HEADS_HERE), :].astype(BF16)
    for half in both:
        stage1(half, 3)
    for half in both:
        landing(side_in.at[half], side_recv.at[half])
        moe_ref[:, half * HALF : (half + 1) * HALF] = (
            side_out[half].astype(F32) + side_in[half].astype(F32)
        ).astype(BF16)

    landing(gathered.at[:, pl.ds(0, 15)], ag_send)
    landing(picked_y, pick_send)
    landing(picked_s, pick_send)
    landing(rows_out.at[pl.ds(0, 3)], land_send)
    for ref in (far2_out, near2_out, far1_out, near1_out):
        landing(ref, ring_send)
    landing(side_out, side_send)


def hand_over_kernel(context_in, moe_in, context_out, moe_out):
    context_out[...] = context_in[...]
    moe_out[...] = moe_in[...]


def per_device(
    queries,
    cache_keys,
    cache_values,
    new_key,
    new_value,
    cache_lengths,
    hidden,
    norm_gain,
    expert_ids,
    router_probs,
    w_gate,
    w_up,
    w_down,
):
    vmem = pl.BlockSpec(memory_space=pltpu.VMEM)
    smem = pl.BlockSpec(memory_space=pltpu.SMEM)
    hbm = pl.BlockSpec(memory_space=pl.ANY)
    dma = pltpu.SemaphoreType.DMA

    def bf16(*shape):
        return pltpu.VMEM(shape, BF16)

    context, moe_out = pl.pallas_call(
        step_kernel,
        out_shape=(
            jax.ShapeDtypeStruct((ROWS, HEADS_HERE * HEAD_DIM), BF16),
            jax.ShapeDtypeStruct((ROWS, D), BF16),
        ),
        in_specs=[vmem] * 4 + [smem] + [vmem] * 3 + [hbm] * 5,
        out_specs=(vmem, vmem),
        scratch_shapes=[
            bf16(2, BLOCKS, ROWS, WIDE),
            bf16(2, BLOCKS, 2, SLOTS, HALF),
            bf16(2, BLOCKS, SLOTS, HALF),
            bf16(GROUPS, BLOCKS, SLOTS, D),
            bf16(2, BLOCKS, ROWS, GROUPS * SLOTS),
            bf16(D, HIDDEN),
            bf16(D, HIDDEN),
            bf16(HIDDEN, D),
            bf16(BLOCKS * SLOTS, HIDDEN),
            bf16(GROUPS, BLOCKS, SLOTS, D),
            bf16(2, BLOCKS, 3, SLOTS, HALF),
            bf16(2, 4, ROWS, HALF),
            bf16(2, 4, 2, ROWS, HALF),
            bf16(2, 4, 2, ROWS // 2, HALF),
            bf16(2, 4, 2, ROWS, HALF),
            bf16(2, ROWS, HALF),
            bf16(2, 2, ROWS, HALF),
            bf16(2, 2, ROWS // 2, HALF),
            bf16(2, 2, ROWS, HALF),
            bf16(2, ROWS, HALF),
            bf16(2, ROWS, HALF),
            bf16(2, CHUNK, KEYS, 2 * HEAD_DIM),
            bf16(2, CHUNK, KEYS, 2 * HEAD_DIM),
            pltpu.VMEM((ROWS * HEADS_HERE, HEAD_DIM), F32),
            pltpu.VMEM((ROWS * HEADS_HERE, HEAD_DIM), F32),
            dma, dma((2, 20)), dma, dma((2,)), dma((3,)), dma((2, 2)),
            dma, dma((2, BLOCKS)), dma, dma((2, 4, 2)), dma((2, 4, 2)), dma((2, 2)), dma((2, 2)), dma, dma((2,)),
        ],
        compiler_params=pltpu.CompilerParams(
            collective_id=0, has_side_effects=True, vmem_limit_bytes=58 * 1024 * 1024
        ),
        name="step",
    )(
        hidden, norm_gain.reshape(D // TAIL, TAIL), expert_ids.T, router_probs.T, cache_lengths,
        queries, new_key, new_value,
        cache_keys, cache_values, w_gate[0], w_up[0], w_down[0],
    )
    return pl.pallas_call(
        hand_over_kernel,
        out_shape=(jax.ShapeDtypeStruct(context.shape, BF16), jax.ShapeDtypeStruct(moe_out.shape, BF16)),
        in_specs=[vmem] * 2,
        out_specs=(vmem, vmem),
        name="hand_over",
    )(context, moe_out)


def solution(mesh):
    in_specs = (
        P("dev", "side"),
        P("dev", None, "side"),
        P("dev", None, "side"),
        P("dev", "side"),
        P("dev", "side"),
        P("dev"),
        P("dev", None),
        P(),
        P("dev", None),
        P("dev", None),
        P("dev", None, "side"),
        P("dev", None, "side"),
        P("dev", "side", None),
    )
    out_specs = (P("dev", "side"), P("dev", None))
    return jax.shard_map(
        per_device, mesh=mesh, in_specs=in_specs, out_specs=out_specs, check_vma=False
    )
```

```python
import functools

import jax
import jax.numpy as jnp
from jax import lax
from jax.experimental import pallas as pl
from jax.experimental.pallas import tpu as pltpu
from jax.sharding import PartitionSpec as P

HEADS = 64
KV_HEADS = 4
HEAD_DIM = 128
RING = 4
BLOCKS = 16
ROWS = 32
SLOTS = 8
GROUPS = 4
D = 4096
HALF = 2048
TAIL = 128
WIDE = HALF + TAIL
MESH = pl.DeviceIdType.MESH
F32 = jnp.float32
BF16 = jnp.bfloat16


class Place:
    def __init__(self):
        self.side = lax.axis_index("side")
        dev = lax.axis_index("dev")
        self.dev = dev
        self.core = dev % 2
        self.x = (dev // 2) % RING
        self.z = (dev // 8) % RING
        self.lo = dev // 32
        self.y = self.side * 2 + self.lo

    @staticmethod
    def index(lo, z, x, core):
        return ((lo * RING + z) * RING + x) * 2 + core

    def plane(self, axis, step):
        if axis == "x":
            return (self.side, self.index(self.lo, self.z, (self.x + step) % RING, self.core))
        return (self.side, self.index(self.lo, (self.z + step) % RING, self.x, self.core))

    def along_y(self, step, core):
        y = (self.y + step) % RING
        return (y // 2, self.index(y % 2, self.z, self.x, core))

    def sibling(self):
        return (self.side, self.index(self.lo, self.z, self.x, 1 - self.core))

    def block(self, half, first, second):
        if half == 0:
            x, z = (self.x + first) % RING, (self.z + second) % RING
        else:
            z, x = (self.z + first) % RING, (self.x + second) % RING
        return z * RING + x


AXES = (("x", "z"), ("z", "x"))
NEAR = (0, -1, 1, 2)
LISTED = (
    (2, 2), (1, 2), (2, 1), (-1, 2), (2, -1), (1, 1), (0, 2), (2, 0),
    (1, -1), (-1, 1), (-1, -1), (0, 1), (1, 0), (0, -1), (-1, 0), (0, 0),
)


def listed(half, first, second):
    return LISTED.index((first, second) if half == 0 else (second, first))


def routing_table(ids_ref, probs_ref):
    place = lax.broadcasted_iota(jnp.int32, (TAIL, ROWS), 0)
    expert = place % 64
    ids = ids_ref[...]
    probs = probs_ref[...]
    share = probs / jnp.sum(probs, axis=0, keepdims=True)
    hit = jnp.zeros((TAIL, ROWS), F32)
    gate = jnp.zeros((TAIL, ROWS), F32)
    for k in range(ids.shape[0]):
        match = ids[k : k + 1, :] == expert
        hit = jnp.where(match, 1.0, hit)
        gate = jnp.where(match, share[k : k + 1, :], gate)
    row = lax.broadcasted_iota(jnp.int32, (ROWS, ROWS), 0)
    col = lax.broadcasted_iota(jnp.int32, (ROWS, ROWS), 1)
    before = jnp.where(row < col, 1.0, 0.0).astype(BF16)
    same = jnp.where(row == col, 1.0, 0.0).astype(BF16)
    rank = jnp.dot(hit.astype(BF16), before, preferred_element_type=F32)
    rank = jnp.where(hit > 0.5, rank, 100.0)
    lead = gate.astype(BF16).astype(F32)
    first = place < 64
    return tuple(
        lax.dot_general(
            same, jnp.where(first, rank, part).astype(BF16), (((1,), (1,)), ((), ())), preferred_element_type=F32
        ).astype(BF16)
        for part in (lead, gate - lead)
    )


CHUNK = 4
KEYS = 256
HEADS_HERE = 32
HIDDEN = 768


def step_kernel(
    hidden_ref, gain_ref, ids_ref, probs_ref, lengths_ref, queries_ref, new_key_ref, new_value_ref,
    keys_hbm, values_hbm, w_gate_hbm, w_up_hbm, w_down_hbm,
    context_ref, moe_ref,
    gathered, picked_y, picked_s, rows_in, weights, w_gate, w_up, w_down, active, rows_out,
    landed, far2_out, near2_out, far2_in, near2_in, far1_out, near1_out, far1_in, near1_in,
    side_out, side_in, keys, values, query_rows, context_rows,
    ag_send, ag_recv, pick_send, rows_recv, w_sem, kv_sem,
    land_send, land_recv, ring_send, far2_recv, near2_recv, far1_recv, near1_recv, side_send, side_recv,
):
    me = Place()
    both = range(2)
    lo = 1 - me.lo
    own_group = me.lo * 2 + me.core
    other_side = (1 - me.side, me.dev)

    w_copies = [
        pltpu.make_async_copy(w_gate_hbm, w_gate, w_sem.at[0]),
        pltpu.make_async_copy(w_up_hbm, w_up, w_sem.at[1]),
        pltpu.make_async_copy(w_down_hbm, w_down, w_sem.at[2]),
    ]

    def cache_copies(chunk):
        tokens = pl.ds(chunk * CHUNK, CHUNK)
        slot = chunk % 2
        return (
            pltpu.make_async_copy(keys_hbm.at[tokens], keys.at[slot], kv_sem.at[slot, 0]),
            pltpu.make_async_copy(values_hbm.at[tokens], values.at[slot], kv_sem.at[slot, 1]),
        )

    for chunk in range(2):
        for copy in cache_copies(chunk):
            copy.start()
    for copy in w_copies:
        copy.start()

    neighbours = (
        [me.plane(axis, step) for axis in ("x", "z") for step in (-1, 1)]
        + [me.along_y(step, core) for step in (-1, 1) for core in (0, 1)]
        + [me.sibling(), other_side]
    )
    barrier = pltpu.get_barrier_semaphore()
    for device in neighbours:
        pl.semaphore_signal(barrier, inc=1, device_id=device, device_id_type=MESH)

    wide = hidden_ref[...].astype(F32)
    inverse = lax.rsqrt(jnp.mean(wide * wide, axis=1, keepdims=True) + 1e-06)
    gain = gain_ref[...].astype(F32)
    tables = routing_table(ids_ref, probs_ref)
    own_block = me.block(0, 0, 0)
    for part in range(D // TAIL):
        half, low = divmod(part * TAIL, HALF)
        normed = wide[:, part * TAIL : (part + 1) * TAIL] * inverse * gain[part : part + 1, :]
        gathered[half, own_block, :, low : low + TAIL] = normed.astype(BF16)
    for half in both:
        gathered[half, own_block, :, HALF:WIDE] = tables[half]

    experts = (
        me.dev,
        me.index(me.lo, me.z, me.x, 1 - me.core),
        me.index(lo, me.z, me.x, 0),
        me.index(lo, me.z, me.x, 1),
    )
    slot_of = lax.broadcasted_iota(jnp.int32, (GROUPS * SLOTS, TAIL), 0)
    lane = lax.broadcasted_iota(jnp.int32, (GROUPS * SLOTS, TAIL), 1)
    wanted = jnp.zeros((GROUPS * SLOTS, TAIL), jnp.int32)
    for j in range(GROUPS):
        wanted = jnp.where(slot_of // SLOTS == j, experts[j], wanted)
    pick_rank = jnp.where(lane == wanted, 1.0, 0.0).astype(BF16)
    pick_gate = jnp.where(lane == wanted + 64, 1.0, 0.0).astype(BF16)
    pick_both = jnp.concatenate([pick_rank, pick_gate], axis=0)

    pl.semaphore_wait(barrier, len(neighbours))

    def hop(half, block, rows, stage, step, sem):
        ref = gathered.at[half, block, rows]
        return pltpu.make_async_remote_copy(
            src_ref=ref, dst_ref=ref, send_sem=ag_send, recv_sem=ag_recv.at[half, sem],
            device_id=me.plane(AXES[half][stage], step), device_id_type=MESH,
        )

    full, low_rows, high_rows = pl.ds(0, ROWS), pl.ds(0, ROWS // 2), pl.ds(ROWS // 2, ROWS // 2)

    def send_both(half, first, stage, base):
        block = me.block(half, first, 0)
        hop(half, block, full, stage, 1, base).start()
        hop(half, block, full, stage, -1, base + 1).start()

    def landing(ref, sem):
        pltpu.make_async_copy(ref, ref, sem).wait()

    def take_full(half, first, stage, base):
        for step, rows, sem in ((-1, low_rows, base), (1, high_rows, base + 1)):
            block = me.block(half, step, 0) if stage == 0 else me.block(half, first, step)
            landing(gathered.at[half, block], ag_recv.at[half, sem])
            hop(half, block, rows, stage, -step, sem + 2).start()

    def take_far(half, first, stage, base):
        block = me.block(half, 2, 0) if stage == 0 else me.block(half, first, 2)
        landing(gathered.at[half, block, low_rows], ag_recv.at[half, base + 2])
        landing(gathered.at[half, block, high_rows], ag_recv.at[half, base + 3])

    def select(half, first, second):
        block = me.block(half, first, second)
        table = gathered[half, block, :, HALF:WIDE]
        rank = lax.dot_general(pick_rank, table, (((1,), (1,)), ((), ())), preferred_element_type=F32)
        slot = (lax.broadcasted_iota(jnp.int32, (GROUPS * SLOTS, ROWS), 0) % SLOTS).astype(F32)
        hot = jnp.where(rank == slot, 1.0, 0.0).astype(BF16)
        both_ways = lax.dot_general(table, pick_both, (((1,), (1,)), ((), ())), preferred_element_type=F32)
        slot = (lax.broadcasted_iota(jnp.int32, (ROWS, GROUPS * SLOTS), 1) % SLOTS).astype(F32)
        weights[half, listed(half, first, second)] = jnp.where(
            both_ways[:, 0 : GROUPS * SLOTS] == slot, both_ways[:, GROUPS * SLOTS :], 0.0
        ).astype(BF16)
        chosen = jnp.dot(hot, gathered[half, block, :, 0:HALF], preferred_element_type=F32).astype(BF16)
        columns = pl.ds(half * HALF, HALF)
        place = listed(half, first, second)
        for core in range(2):
            picked_y[half, block, core] = chosen[16 + 8 * core : 24 + 8 * core]
            pltpu.make_async_remote_copy(
                src_ref=picked_y.at[half, block, core],
                dst_ref=rows_in.at[own_group, place, :, columns],
                send_sem=pick_send, recv_sem=rows_recv.at[1],
                device_id=me.along_y(1 if half == 0 else -1, core), device_id_type=MESH,
            ).start()
        picked_s[half, block] = chosen[8:16]
        pltpu.make_async_remote_copy(
            src_ref=picked_s.at[half, block],
            dst_ref=rows_in.at[own_group, place, :, columns],
            send_sem=pick_send, recv_sem=rows_recv.at[0],
            device_id=me.sibling(), device_id_type=MESH,
        ).start()
        rows_in[own_group, place, :, columns] = chosen[0:8]

    def attend(chunk):
        slot = chunk % 2
        for copy in cache_copies(chunk):
            copy.wait()
        scale = HEAD_DIM ** (-0.5)
        position = lax.broadcasted_iota(jnp.int32, (HEADS_HERE, KEYS), 1)
        upper = lax.broadcasted_iota(jnp.int32, (HEADS_HERE, HEAD_DIM), 0) < HEADS_HERE // 2

        def by_group(row):
            return jnp.where(upper, row[:, 0:HEAD_DIM], row[:, HEAD_DIM:])

        for item in range(CHUNK):
            token = chunk * CHUNK + item
            heads = slice(token * HEADS_HERE, (token + 1) * HEADS_HERE)
            query = query_rows[heads]
            split = jnp.concatenate([jnp.where(upper, query, 0.0), jnp.where(upper, 0.0, query)], axis=1)
            scores = lax.dot_general(
                split.astype(BF16), keys[slot, item], (((1,), (1,)), ((), ())), preferred_element_type=F32
            )
            scores = jnp.where(position < lengths_ref[token], scores * scale, -1e30)
            own_key = by_group(new_key_ref[token : token + 1, :].astype(F32))
            own = jnp.sum(query * own_key, axis=1, keepdims=True) * scale
            top = jnp.maximum(jnp.max(scores, axis=1, keepdims=True), own)
            scores = jnp.exp(scores - top)
            own = jnp.exp(own - top)
            share = 1.0 / (jnp.sum(scores, axis=1, keepdims=True) + own)
            probs = (scores * share).astype(BF16)
            own = (own * share).astype(BF16).astype(F32)
            mixed = by_group(jnp.dot(probs, values[slot, item], preferred_element_type=F32))
            context_rows[heads] = mixed + own * by_group(new_value_ref[token : token + 1, :].astype(F32))
        if chunk + 2 < ROWS // CHUNK:
            for copy in cache_copies(chunk + 2):
                copy.start()

    for half in both:
        send_both(half, 0, 0, 0)
    for half in both:
        send_both(half, 0, 1, 4)
    for half in both:
        select(half, 0, 0)
    for head in range(HEADS_HERE):
        lanes = slice(head * HEAD_DIM, (head + 1) * HEAD_DIM)
        query_rows[pl.ds(head, ROWS, stride=HEADS_HERE), :] = queries_ref[:, lanes].astype(F32)
    attend(0)
    attend(1)
    for half in both:
        take_full(half, 0, 0, 0)
        send_both(half, -1, 1, 8)
    for half in both:
        select(half, -1, 0)
        select(half, 1, 0)
    attend(2)
    for half in both:
        take_full(half, 0, 1, 4)
        send_both(half, 1, 1, 12)
    for half in both:
        take_far(half, 0, 0, 0)
    for half in both:
        select(half, 2, 0)
        select(half, 0, -1)
        select(half, 0, 1)
    attend(3)
    for index in range(1, 4):
        first = NEAR[index]
        for half in both:
            take_full(half, first, 1, 4 + 4 * index)
            if index == 1:
                send_both(half, 2, 1, 16)
        for half in both:
            take_far(half, NEAR[index - 1], 1, 4 * index)
        for half in both:
            select(half, first, -1)
            select(half, first, 1)
            select(half, NEAR[index - 1], 2)
        if index < 3:
            attend(3 + index)
    for half in both:
        take_far(half, 2, 1, 16)
        select(half, 2, 2)
    PART = BLOCKS // 2

    def expert(base, part):
        rows = rows_in[pl.ds(base, 2), part * PART : (part + 1) * PART].reshape(2 * PART * SLOTS, D)
        for low in range(0, HIDDEN, 256):
            columns = slice(low, low + 256)
            gate = jnp.dot(rows, w_gate[:, columns], preferred_element_type=F32)
            up = jnp.dot(rows, w_up[:, columns], preferred_element_type=F32)
            active[:, columns] = (gate / (1.0 + jnp.exp(-gate)) * up).astype(BF16)

    def expert_down(base, part, half):
        for low in range(half * HALF, (half + 1) * HALF, 512):
            columns = slice(low, low + 512)
            out = jnp.dot(active[...], w_down[:, columns], preferred_element_type=F32).astype(BF16)
            rows_out[pl.ds(base, 2), part * PART : (part + 1) * PART, :, columns] = out.reshape(2, PART, SLOTS, 512)

    far_order = (2, 1, -1, 0)
    visits = (
        (2, 2), (1, 2), (2, 1), (2, -1), (-1, 2), (1, 1), (1, -1), (2, 0),
        (0, 2), (-1, 1), (-1, -1), (1, 0), (0, 1), (0, -1), (-1, 0), (0, 0),
    )

    def give_y(half, visit):
        place = listed(half, *visits[visit])
        columns = pl.ds(half * HALF, HALF)
        for core in range(2):
            pltpu.make_async_remote_copy(
                src_ref=rows_out.at[lo * 2 + core, place, :, columns],
                dst_ref=landed.at[half, visit, 1 + me.core],
                send_sem=land_send, recv_sem=land_recv.at[half, visit],
                device_id=me.along_y(1 if half == 0 else -1, core), device_id_type=MESH,
            ).start()

    def give_sibling(half, visit):
        place = listed(half, *visits[visit])
        pltpu.make_async_remote_copy(
            src_ref=rows_out.at[me.lo * 2 + 1 - me.core, place, :, pl.ds(half * HALF, HALF)],
            dst_ref=landed.at[half, visit, 0],
            send_sem=land_send, recv_sem=land_recv.at[half, visit],
            device_id=me.sibling(), device_id_type=MESH,
        ).start()

    AHEAD = 6
    for copy in w_copies:
        copy.wait()
    landing(rows_in.at[0], rows_recv.at[0])
    expert(me.lo * 2, 0)
    for half in both:
        expert_down(me.lo * 2, 0, half)
    landing(rows_in.at[pl.ds(0, 2)], rows_recv.at[1])
    expert(lo * 2, 0)
    for half in both:
        expert_down(lo * 2, 0, half)
        for visit in range(AHEAD):
            give_y(half, visit)
            give_sibling(half, visit)
    for base in (lo * 2, me.lo * 2):
        expert(base, 1)
        for half in both:
            expert_down(base, 1, half)

    turn = [0, 0]

    def mixed(half, first, second):
        assert visits[turn[half]] == (first, second)
        if turn[half] + AHEAD < BLOCKS:
            give_y(half, turn[half] + AHEAD)
            give_sibling(half, turn[half] + AHEAD)
        visit = turn[half]
        turn[half] += 1
        place = listed(half, first, second)
        landing(landed.at[half, visit], land_recv.at[half, visit])
        own = rows_out[own_group, place, :, half * HALF : (half + 1) * HALF]
        parts = landed[half, visit]
        rows = jnp.concatenate([own, parts[0], parts[1], parts[2]], axis=0)
        return jnp.dot(weights[0, place], rows, preferred_element_type=F32) + jnp.dot(
            weights[1, place], rows, preferred_element_type=F32
        )

    def ring(half, stage, step, src, dst, sem):
        pltpu.make_async_remote_copy(
            src_ref=src, dst_ref=dst, send_sem=ring_send, recv_sem=sem,
            device_id=me.plane(AXES[half][stage], step), device_id_type=MESH,
        ).start()

    low, high = slice(0, ROWS // 2), slice(ROWS // 2, ROWS)

    def send_far(half, stage, value, out, into, sems):
        out[...] = value.astype(BF16)
        for way, step, rows in ((0, 1, low_rows), (1, -1, high_rows)):
            ring(half, stage, step, out.at[rows], into.at[way], sems(way))

    def send_near(half, stage, way, value, far_in, far_sem, out, into, sem):
        landing(far_in, far_sem)
        passed = far_in[...].astype(F32)
        if way == 0:
            out[low] = (value[low] + passed).astype(BF16)
            out[high] = value[high].astype(BF16)
        else:
            out[low] = value[low].astype(BF16)
            out[high] = (value[high] + passed).astype(BF16)
        ring(half, stage, 1 if way == 0 else -1, out, into, sem)

    def far2(half, index):
        value = mixed(half, far_order[index], 2)
        send_far(
            half, 1, value, far2_out.at[half, index], far2_in.at[half, index],
            lambda way: far2_recv.at[half, index, way],
        )

    def near2(half, index):
        for way, second in ((0, 1), (1, -1)):
            value = mixed(half, far_order[index], second)
            send_near(
                half, 1, way, value, far2_in.at[half, index, way], far2_recv.at[half, index, way],
                near2_out.at[half, index, way], near2_in.at[half, index, way], near2_recv.at[half, index, way],
            )

    def stage1(half, index):
        value = mixed(half, far_order[index], 0)
        for way in both:
            landing(near2_in.at[half, index, way], near2_recv.at[half, index, way])
            value = value + near2_in[half, index, way].astype(F32)
        first = far_order[index]
        if first == 2:
            send_far(half, 0, value, far1_out.at[half], far1_in.at[half], lambda way: far1_recv.at[half, way])
        elif first != 0:
            way = 0 if first == 1 else 1
            send_near(
                half, 0, way, value, far1_in.at[half, way], far1_recv.at[half, way],
                near1_out.at[half, way], near1_in.at[half, way], near1_recv.at[half, way],
            )
        else:
            for way in both:
                landing(near1_in.at[half, way], near1_recv.at[half, way])
                value = value + near1_in[half, way].astype(F32)
            side_out[half] = value.astype(BF16)
            pltpu.make_async_remote_copy(
                src_ref=side_out.at[half], dst_ref=side_in.at[half],
                send_sem=side_send, recv_sem=side_recv.at[half],
                device_id=other_side, device_id_type=MESH,
            ).start()

    for half in both:
        far2(half, 0)
    for index in range(4):
        if index < 3:
            for half in both:
                far2(half, index + 1)
        for half in both:
            near2(half, index)
        if index > 0:
            for half in both:
                stage1(half, index - 1)
        if index == 1:
            attend(6)
        elif index == 2:
            attend(7)
    for head in range(HEADS_HERE):
        lanes = slice(head * HEAD_DIM, (head + 1) * HEAD_DIM)
        context_ref[:, lanes] = context_rows[pl.ds(head, ROWS, stride=HEADS_HERE), :].astype(BF16)
    for half in both:
        stage1(half, 3)
    for half in both:
        landing(side_in.at[half], side_recv.at[half])
        moe_ref[:, half * HALF : (half + 1) * HALF] = (
            side_out[half].astype(F32) + side_in[half].astype(F32)
        ).astype(BF16)

    landing(gathered.at[:, pl.ds(0, 15)], ag_send)
    landing(picked_y, pick_send)
    landing(picked_s, pick_send)
    landing(rows_out.at[pl.ds(0, 3)], land_send)
    for ref in (far2_out, near2_out, far1_out, near1_out):
        landing(ref, ring_send)
    landing(side_out, side_send)


def hand_over_kernel(context_in, moe_in, context_out, moe_out):
    context_out[...] = context_in[...]
    moe_out[...] = moe_in[...]


def per_device(
    queries,
    cache_keys,
    cache_values,
    new_key,
    new_value,
    cache_lengths,
    hidden,
    norm_gain,
    expert_ids,
    router_probs,
    w_gate,
    w_up,
    w_down,
):
    vmem = pl.BlockSpec(memory_space=pltpu.VMEM)
    smem = pl.BlockSpec(memory_space=pltpu.SMEM)
    hbm = pl.BlockSpec(memory_space=pl.ANY)
    dma = pltpu.SemaphoreType.DMA

    def bf16(*shape):
        return pltpu.VMEM(shape, BF16)

    context, moe_out = pl.pallas_call(
        step_kernel,
        out_shape=(
            jax.ShapeDtypeStruct((ROWS, HEADS_HERE * HEAD_DIM), BF16),
            jax.ShapeDtypeStruct((ROWS, D), BF16),
        ),
        in_specs=[vmem] * 4 + [smem] + [vmem] * 3 + [hbm] * 5,
        out_specs=(vmem, vmem),
        scratch_shapes=[
            bf16(2, BLOCKS, ROWS, WIDE),
            bf16(2, BLOCKS, 2, SLOTS, HALF),
            bf16(2, BLOCKS, SLOTS, HALF),
            bf16(GROUPS, BLOCKS, SLOTS, D),
            bf16(2, BLOCKS, ROWS, GROUPS * SLOTS),
            bf16(D, HIDDEN),
            bf16(D, HIDDEN),
            bf16(HIDDEN, D),
            bf16(BLOCKS * SLOTS, HIDDEN),
            bf16(GROUPS, BLOCKS, SLOTS, D),
            bf16(2, BLOCKS, 3, SLOTS, HALF),
            bf16(2, 4, ROWS, HALF),
            bf16(2, 4, 2, ROWS, HALF),
            bf16(2, 4, 2, ROWS // 2, HALF),
            bf16(2, 4, 2, ROWS, HALF),
            bf16(2, ROWS, HALF),
            bf16(2, 2, ROWS, HALF),
            bf16(2, 2, ROWS // 2, HALF),
            bf16(2, 2, ROWS, HALF),
            bf16(2, ROWS, HALF),
            bf16(2, ROWS, HALF),
            bf16(2, CHUNK, KEYS, 2 * HEAD_DIM),
            bf16(2, CHUNK, KEYS, 2 * HEAD_DIM),
            pltpu.VMEM((ROWS * HEADS_HERE, HEAD_DIM), F32),
            pltpu.VMEM((ROWS * HEADS_HERE, HEAD_DIM), F32),
            dma, dma((2, 20)), dma, dma((2,)), dma((3,)), dma((2, 2)),
            dma, dma((2, BLOCKS)), dma, dma((2, 4, 2)), dma((2, 4, 2)), dma((2, 2)), dma((2, 2)), dma, dma((2,)),
        ],
        compiler_params=pltpu.CompilerParams(
            collective_id=0, has_side_effects=True, vmem_limit_bytes=58 * 1024 * 1024
        ),
        name="step",
    )(
        hidden, norm_gain.reshape(D // TAIL, TAIL), expert_ids.T, router_probs.T, cache_lengths,
        queries, new_key, new_value,
        cache_keys, cache_values, w_gate[0], w_up[0], w_down[0],
    )
    return pl.pallas_call(
        hand_over_kernel,
        out_shape=(jax.ShapeDtypeStruct(context.shape, BF16), jax.ShapeDtypeStruct(moe_out.shape, BF16)),
        in_specs=[vmem] * 2,
        out_specs=(vmem, vmem),
        name="hand_over",
    )(context, moe_out)


def solution(mesh):
    in_specs = (
        P("dev", "side"),
        P("dev", None, "side"),
        P("dev", None, "side"),
        P("dev", "side"),
        P("dev", "side"),
        P("dev"),
        P("dev", None),
        P(),
        P("dev", None),
        P("dev", None),
        P("dev", None, "side"),
        P("dev", None, "side"),
        P("dev", "side", None),
    )
    out_specs = (P("dev", "side"), P("dev", None))
    return jax.shard_map(
        per_device, mesh=mesh, in_specs=in_specs, out_specs=out_specs, check_vma=False
    )
```
